768 devices in a mesh: gx: 16 (over x, y_lo), gy: 48 (over y_hi, z, core).
Axes of the slice: x: 4, y: 8 (y_hi: 2, y_lo: 4; y = y_hi * 4 + y_lo), z: 12, core: 2. Of those that a mesh axis runs over, the one named last changes fastest.
Arguments:
- spin_angles: float32 [2, 2, 4, 1536, 2048], P(None, None, None, 'gy', 'gx'), may hold values from -3.1415927 to 3.1415927, as said below
- species: int32 [2, 4, 1536, 2048], P(None, None, 'gy', 'gx'), may hold values 0 or 1
Outputs:
- spins_next: float32 [2, 3, 4, 1536, 2048], P(None, None, None, 'gy', 'gx')
- dipole_field: float32 [3, 1, 384, 512], P(None, None, 'gy', 'gx')
The draws below stay inside these ranges and needn't reach their ends.
Inputs may be any that keep to these rules, and one draw needn't show every extreme that they name: `spin_angles`: along dimension 1 the first entry is the polar angle, from 0 to pi, and the second the azimuth. `species`: 0 marks an iron atom and 1 a cobalt atom.
All inputs are finite; a program needn't handle non-finite values. No bound on the sum of `species` on one device may be relied on, other than what follows from the above.
Results may differ from the reference program's by a relative error of at most 0.000075.
Values sent between devices are 32-bit elements; how exact they have to be, the bound alone decides.
A program may use at most 64 MiB of HBM per device.

```python
import math
import jax
import jax.numpy as jnp
from jax import lax

MZ = 1
CELLS_M = 4
AZ = 4
MX = 512
MY = 384
NXA = 2048
NYA = 1536


def draw_spin_angles(key, part):
    polar_key, azimuth_key = jax.random.split(key)
    array_shape = (2, 1, AZ, NYA, NXA)
    polar_angle = jax.random.uniform(polar_key, array_shape, jnp.float32, 0.0, math.pi)
    azimuth = jax.random.uniform(azimuth_key, array_shape, jnp.float32, -math.pi, math.pi)
    return jnp.concatenate([polar_angle, azimuth], axis=1)


def with_ends(entries, own_key, least, top_value):
    dims = entries.shape
    place = [jax.random.randint(jax.random.fold_in(own_key, axis), (), 0, dims[axis]) for axis in range(len(dims))]
    entries = entries.at[tuple(place)].set(least)
    longest = dims.index(max(dims))
    place[longest] = (place[longest] + 1) % dims[longest]
    return entries.at[tuple(place)].set(top_value)


def setup_inputs(seed: int = 0) -> dict:
    key_list = jax.random.split(jax.random.key(seed), 3)
    spin_angles = draw_spin_angles(jax.random.fold_in(key_list[2], 71), 0)
    species = with_ends((jax.random.randint(key_list[1], (2, AZ, NYA, NXA), 0, 2) < 1).astype(jnp.int32), jax.random.fold_in(key_list[1], 1), 0, 1)
    return dict(spin_angles=spin_angles, species=species)


DAMPING = 0.1
TIME_STEP = 0.05
EXCHANGE_SCALE = 0.6
DIPOLE = 2.0
MOMENT_PAIR = (2.22, 1.72)
COUPLING_PAIR = (1.0, 1.25)
ANISOTROPY_PAIR = (0.3, 0.9)

def species_value(species, table_pair):
    return jnp.where(species == 1, table_pair[1], table_pair[0]).astype(jnp.float32)

def unit_vectors(angles):
    polar_angle = angles[:, 0]
    azimuth = angles[:, 1]
    radial = jnp.sin(polar_angle)
    return jnp.stack([radial * jnp.cos(azimuth), radial * jnp.sin(azimuth), jnp.cos(polar_angle)], axis=1)

def box_sum(padded):
    along_x = padded[..., :-1] + padded[..., 1:]
    along_y = along_x[..., :-1, :] + along_x[..., 1:, :]
    return along_y[..., :-1, :, :] + along_y[..., 1:, :, :]

def neighbour_sums(padded):
    corner_side = box_sum(padded[1])[:, :-1, :-1, :-1]
    centre_side = box_sum(padded[0])[:, 1:, 1:, 1:]
    return jnp.stack([corner_side, centre_side])

def cross_product(left_side, right_side):
    return jnp.stack([left_side[:, 1] * right_side[:, 2] - left_side[:, 2] * right_side[:, 1], left_side[:, 2] * right_side[:, 0] - left_side[:, 0] * right_side[:, 2], left_side[:, 0] * right_side[:, 1] - left_side[:, 1] * right_side[:, 0]], axis=1)

def torque(vectors, field_total):
    precess = cross_product(vectors, field_total)
    relaxation = cross_product(vectors, precess)
    return -(precess + DAMPING * relaxation) / (1.0 + DAMPING * DAMPING)

def normalized(vectors):
    return vectors / jnp.sqrt(lax.optimization_barrier(jnp.sum(vectors * vectors, axis=1, keepdims=True)))

def total_field(vectors, neighbour_term, exchange_ratio, easy_axis, dipole_atoms):
    along_z = easy_axis * vectors[:, 2]
    zero_part = jnp.zeros_like(along_z)
    field_total = EXCHANGE_SCALE * exchange_ratio[:, None] * neighbour_term + dipole_atoms[None]
    return field_total + jnp.stack([zero_part, zero_part, along_z], axis=1)

def spread_cells(cell_values, repeat):
    dims_in = cell_values.shape
    expanded = jnp.broadcast_to(cell_values[:, :, None, :, None, :, None], (dims_in[0], dims_in[1], repeat, dims_in[2], repeat, dims_in[3], repeat))
    return expanded.reshape(dims_in[0], dims_in[1] * repeat, dims_in[2] * repeat, dims_in[3] * repeat)

def wave_numbers(indices, period):
    wrapped = jnp.where(indices < period // 2, indices, indices - period)
    return wrapped.astype(jnp.float32) * (2.0 * math.pi / period)

def apply_kernel(real_part, imag_part, wave_x, wave_y):
    layer_count = real_part.shape[1]
    square = wave_x * wave_x + wave_y * wave_y
    length = jnp.sqrt(square)
    inverse = jnp.where(square > 0, 1.0 / jnp.where(square > 0, length, 1.0), 0.0)
    proj_real = wave_x * real_part[0] + wave_y * real_part[1]
    proj_imag = wave_x * imag_part[0] + wave_y * imag_part[1]
    zero_grid = jnp.zeros(proj_real.shape[1:], real_part.dtype)
    rows_real = []
    rows_imag = []
    for target in range(layer_count):
        x_real, x_imag, y_real, y_imag, z_real, z_imag = (zero_grid, zero_grid, zero_grid, zero_grid, zero_grid, zero_grid)
        for source in range(layer_count):
            layer_gap = target - source
            falloff = 0.5 * jnp.exp(-float(abs(layer_gap)) * length)
            lateral = inverse * falloff
            x_real = x_real - wave_x * lateral * proj_real[source]
            x_imag = x_imag - wave_x * lateral * proj_imag[source]
            y_real = y_real - wave_y * lateral * proj_real[source]
            y_imag = y_imag - wave_y * lateral * proj_imag[source]
            normal_part = length * falloff - (1.0 if layer_gap == 0 else 0.0)
            z_real = z_real + normal_part * real_part[2, source]
            z_imag = z_imag + normal_part * imag_part[2, source]
            if layer_gap != 0:
                signed = (1.0 if layer_gap > 0 else -1.0) * falloff
                x_real = x_real + signed * wave_x * imag_part[2, source]
                x_imag = x_imag - signed * wave_x * real_part[2, source]
                y_real = y_real + signed * wave_y * imag_part[2, source]
                y_imag = y_imag - signed * wave_y * real_part[2, source]
                z_real = z_real + signed * proj_imag[source]
                z_imag = z_imag - signed * proj_real[source]
        rows_real.append(jnp.stack([x_real, y_real, z_real]))
        rows_imag.append(jnp.stack([x_imag, y_imag, z_imag]))
    return (jnp.stack(rows_real, axis=1), jnp.stack(rows_imag, axis=1))

def dipole_from_moments(cell_moments):
    size_y = cell_moments.shape[2]
    size_x = cell_moments.shape[3]
    period_y = 2 * size_y
    period_x = 2 * size_x
    padded = jnp.pad(cell_moments, ((0, 0), (0, 0), (0, size_y), (0, size_x)))
    spectrum = jnp.fft.fft2(padded)
    wave_y = wave_numbers(jnp.arange(period_y, dtype=jnp.int32), period_y)[:, None]
    wave_x = wave_numbers(jnp.arange(period_x, dtype=jnp.int32), period_x)[None, :]
    result_real, result_imag = apply_kernel(jnp.real(spectrum), jnp.imag(spectrum), wave_x, wave_y)
    restored = jnp.fft.ifft2(lax.complex(result_real, result_imag))
    return DIPOLE * jnp.real(restored)[:, :, :size_y, :size_x]

def reference(spin_angles, species):
    vectors = unit_vectors(spin_angles)
    moment = species_value(species, MOMENT_PAIR)
    coupling = species_value(species, COUPLING_PAIR)
    exchange_ratio = coupling / moment
    easy_axis = 2.0 * species_value(species, ANISOTROPY_PAIR) / moment
    scaled = (moment[:, None] * vectors).reshape(2, 3, MZ, CELLS_M, MY, CELLS_M, MX, CELLS_M)
    cell_moments = lax.optimization_barrier(jnp.sum(scaled, axis=(0, 3, 5, 7))) / (2 * CELLS_M * CELLS_M * CELLS_M)
    dipole_field = dipole_from_moments(cell_moments)
    dipole_atoms = spread_cells(dipole_field, CELLS_M)

    def neighbours(spin_vecs):
        weighted = coupling[:, None] * spin_vecs
        padded = jnp.pad(weighted, ((0, 0), (0, 0), (1, 1), (1, 1), (1, 1)))
        return neighbour_sums(padded)
    field_first = total_field(vectors, neighbours(vectors), exchange_ratio, easy_axis, dipole_atoms)
    torque_first = torque(vectors, field_first)
    predicted = normalized(vectors + TIME_STEP * torque_first)
    field_second = total_field(predicted, neighbours(predicted), exchange_ratio, easy_axis, dipole_atoms)
    torque_second = torque(predicted, field_second)
    spins_next = normalized(vectors + 0.5 * TIME_STEP * (torque_first + torque_second))
    return (spins_next, dipole_field)
```

```python
import functools
import math

import jax
import jax.numpy as jnp
import numpy as np
from jax import lax
from jax.experimental import pallas as pl
from jax.experimental.pallas import tpu as pltpu
from jax.sharding import PartitionSpec as P

MESH = pl.DeviceIdType.MESH
HIGHEST = lax.Precision.HIGHEST
F32 = jnp.float32

CELLS_M = 4
DAMPING = 0.1
TIME_STEP = 0.05
EXCHANGE_SCALE = 0.6
DIPOLE = 2.0
MOMENT_PAIR = (2.22, 1.72)
COUPLING_PAIR = (1.0, 1.25)
ANISOTROPY_PAIR = (0.3, 0.9)
RATIO_PAIR = (COUPLING_PAIR[0] / MOMENT_PAIR[0], COUPLING_PAIR[1] / MOMENT_PAIR[1])
EASY_PAIR = (2 * ANISOTROPY_PAIR[0] / MOMENT_PAIR[0], 2 * ANISOTROPY_PAIR[1] / MOMENT_PAIR[1])

PART_K = 32
ROWS = 8
COLS = 32
WINDOWS = 10
TABLE_LEAD = 8
TABLE_ROWS = 400


def wave_tables(nx, ny):
    period_x, period_y = 2 * nx * COLS, 2 * ny * ROWS
    half_y = period_y // 2
    v = np.arange(period_x // 2 + 1)
    u = np.arange(half_y + 1)
    a = 2 * np.pi * v[:, None] / period_x
    b = 2 * np.pi * u[None, :] / period_y
    k = np.sqrt(a * a + b * b)
    inv = np.where(k > 0, 1.0 / np.where(k > 0, k, 1.0), 0.0)
    g = {
        "xx": -a * a * 0.5 * inv,
        "yy": -b * b * 0.5 * inv,
        "zz": 0.5 * k - 1.0,
        "xy": -a * b * 0.5 * inv,
    }
    dy = np.arange(-TABLE_LEAD, TABLE_ROWS - TABLE_LEAD)
    angle = 2 * np.pi * ((u[:, None] * dy[None, :]) % period_y) / period_y
    fold = np.where((u == 0) | (u == half_y), 1.0, 2.0)
    cosine = fold[:, None] * np.cos(angle)
    sine = np.where((u == 0) | (u == half_y), 0.0, 2.0)[:, None] * np.sin(angle)
    scale = DIPOLE / (period_x * period_y) * np.where((v == 0) | (v == period_x // 2), 1.0, 2.0)
    tables = [scale[:, None] * (g[n] @ cosine) for n in ("xx", "yy", "zz")]
    odd = scale[:, None] * (g["xy"] @ sine)
    odd[-1] = 0.0
    tables.append(odd)
    lanes = np.stack(tables)
    out = np.zeros((nx + 1, TABLE_ROWS, 4 * PART_K), np.float32)
    for s in range(nx):
        block = lanes[:, s * PART_K : (s + 1) * PART_K, :]
        out[s] = block.transpose(2, 0, 1).reshape(TABLE_ROWS, -1)
    out[nx] = out[0]
    for n in range(4):
        out[nx, :, n * PART_K] = lanes[n, -1, :]
    corner = DIPOLE / (period_x * period_y) * float(-0.5 * np.pi * np.pi / np.sqrt(2 * np.pi**2))
    return out, corner


def trig_tables(nx):
    period = 2 * nx * COLS
    lane = np.arange(128)
    comp = np.where(lane < 96, lane // 32, np.where(lane < 102, (lane - 96) // 2, 3))
    place = np.where(lane < 96, lane % 32, np.where(lane % 2 == 0, -1, 32))
    j = np.arange(PART_K)
    t = 2 * np.pi * ((j[:, None] * place[None, :]) % period) / period
    base = np.stack([np.cos(t), np.sin(t)]).astype(np.float32)
    s = np.arange(nx)
    t = 2 * np.pi * ((s[:, None] * PART_K * place[None, :]) % period) / period
    phase = np.stack([np.cos(t), np.sin(t)], axis=1).astype(np.float32)
    jl = lane % 32
    t = 2 * np.pi * ((s[:, None] * COLS * jl[None, :]) % period) / period
    twist = np.stack([np.cos(t), np.sin(t)]).astype(np.float32)
    row = np.stack([comp, np.where(place % 2 == 0, 1, -1)]).astype(np.float32)
    return base, phase, twist, row


def sine(r):
    q = r * r
    p = 1.0 / 6227020800.0
    for c in (-1.0 / 39916800.0, 1.0 / 362880.0, -1.0 / 5040.0, 1.0 / 120.0, -1.0 / 6.0):
        p = p * q + c
    return r + r * q * p


def sine_cosine(x):
    size = jnp.abs(x)
    far = (np.float32(math.pi) - size) + np.float32(math.pi - float(np.float32(math.pi)))
    s = sine(jnp.where(size > np.float32(math.pi / 2), far, size))
    half = (np.float32(math.pi / 2) - size) + np.float32(
        math.pi / 2 - float(np.float32(math.pi / 2))
    )
    return jnp.where(x < 0, -s, s), sine(half)


def pick(cobalt, pair):
    return jnp.where(cobalt, np.float32(pair[1]), np.float32(pair[0]))


def unit(polar, azimuth):
    sp, cp = sine_cosine(polar)
    sq, cq = sine_cosine(azimuth)
    return sp * cq, sp * sq, cp


def iota(shape, dim):
    return lax.broadcasted_iota(jnp.int32, shape, dim)


def gather_kernel(
    nx, ny, corner,
    ang, spc, table_hbm, base, phase, twist, lanes,
    fld, hy_ang, hy_spc, hx, hc,
    mom, tile, b_a, q_mat, tab, tab2, up, dn, b_b, send_c, b_c, pack, g_ang, g_spc, g_x, g_c,
    tab_sem, s_a, r_a, s_b, r_b, s_c, r_c, s_h, r_h,
):
    gx, gy = lax.axis_index("gx"), lax.axis_index("gy")
    left, right = lax.rem(gx + nx - 1, nx), lax.rem(gx + 1, nx)
    below, above = lax.rem(gy + ny - 1, ny), lax.rem(gy + 1, ny)

    loads = [
        pltpu.make_async_copy(table_hbm.at[gx], tab.at[0], tab_sem.at[0]),
        pltpu.make_async_copy(table_hbm.at[jnp.where(gx == 0, nx, gx)], tab.at[1], tab_sem.at[1]),
    ]
    for load in loads:
        load.start()

    barrier = pltpu.get_barrier_semaphore()

    def hail(device):
        pl.semaphore_signal(barrier, inc=1, device_id=device, device_id_type=MESH)

    @pl.loop(1, ny)
    def _(o):
        hail((gx, lax.rem(gy + o, ny)))

    @pl.loop(1, nx)
    def _(o):
        hail((lax.rem(gx + o, nx), gy))

    for device in ((left, below), (right, below), (left, above), (right, above)):
        hail(device)

    def remote(src, dst, send, recv, device):
        return pltpu.make_async_remote_copy(
            src_ref=src, dst_ref=dst, send_sem=send, recv_sem=recv, device_id=device, device_id_type=MESH
        )

    total = [jnp.zeros((32, 128), F32) for _ in range(3)]
    for sub in range(2):
        for z in range(4):
            moment = pick(spc[sub, z] == 1, MOMENT_PAIR)
            v = unit(ang[sub, 0, z], ang[sub, 1, z])
            total = [t + moment * c for t, c in zip(total, v)]
    x_cell, l_cell = iota((128, 128), 0) >> 2, iota((128, 128), 1)
    packed = jnp.zeros((8, 128), F32)
    for c in range(3):
        mom[c] = total[c]
        rows = mom[c, pl.ds(0, 8, 4), :]
        for r in range(1, 4):
            rows = rows + mom[c, pl.ds(r, 8, 4), :]
        spread = jnp.where(l_cell == x_cell + 32 * c, np.float32(1 / 128), np.float32(0))
        packed = packed + jnp.dot(rows, spread, precision=HIGHEST, preferred_element_type=F32)
    tile[...] = packed

    lane = iota((128, 128), 1)
    edges = jnp.zeros((128, 128), F32)
    for q in range(3):
        for sub in range(2):
            n = 2 * q + sub
            block = ang[sub, q] if q < 2 else spc[sub].astype(F32)
            block = block.reshape(128, 128)
            edges = jnp.where(lane == n, pltpu.roll(block, n, 1) if n else block, edges)
            edges = jnp.where(lane == 8 + n, pltpu.roll(block, n + 9, 1), edges)
    edges = jnp.transpose(edges)
    pack[0] = edges[0:8]
    pack[1] = edges[8:16]

    b_cos, b_sin = base[0], base[1]
    p_cos, p_sin = phase[gx, 0:1, :], phase[gx, 1:2, :]
    cosine = b_cos * p_cos - b_sin * p_sin
    sinus = b_sin * p_cos + b_cos * p_sin
    comp, parity = lanes[0:1, :], lanes[1:2, :]
    single = (iota((32, 128), 0) + gx) == 0
    for c in range(3):
        mine = comp == np.float32(c)
        real, imag = (sinus, cosine) if c == 1 else (cosine, -sinus)
        q_mat[pl.ds(32 * c, 32), :] = jnp.where(mine, jnp.where(single, 1.0, real), 0.0)
        q_mat[pl.ds(128 + 32 * c, 32), :] = jnp.where(mine, jnp.where(single, parity, imag), 0.0)
    q_mat[pl.ds(96, 32), :] = jnp.zeros((32, 128), F32)
    q_mat[pl.ds(224, 32), :] = jnp.zeros((32, 128), F32)

    for load in loads:
        load.wait()
    wide = iota((TABLE_ROWS, 128), 1)
    for p in range(2):
        t = tab[p]
        tab2[p] = jnp.where(
            wide < 32,
            pltpu.roll(t, 32, 1),
            jnp.where(wide < 64, -pltpu.roll(t, 64, 1), 0.0),
        )

    pl.semaphore_wait(barrier, nx - 1 + ny - 1 + 4)

    @pl.loop(1, nx)
    def _(o):
        to = lax.rem(gx + o, nx)
        remote(tile, b_a.at[gx], s_a.at[o], r_a.at[gx], (to, gy)).start()

    halos = [
        remote(ang.at[:, :, :, pl.ds(31, 1), :], g_ang.at[:, :, :, pl.ds(0, 1), :], s_h.at[0], r_h.at[0], (gx, above)),
        remote(ang.at[:, :, :, pl.ds(0, 1), :], g_ang.at[:, :, :, pl.ds(1, 1), :], s_h.at[1], r_h.at[1], (gx, below)),
        remote(spc.at[:, :, pl.ds(31, 1), :], g_spc.at[:, :, pl.ds(0, 1), :], s_h.at[2], r_h.at[2], (gx, above)),
        remote(spc.at[:, :, pl.ds(0, 1), :], g_spc.at[:, :, pl.ds(1, 1), :], s_h.at[3], r_h.at[3], (gx, below)),
        remote(pack.at[1], g_x.at[0], s_h.at[4], r_h.at[4], (right, gy)),
        remote(pack.at[0], g_x.at[1], s_h.at[5], r_h.at[5], (left, gy)),
        remote(pack.at[1], g_c.at[0], s_h.at[6], r_h.at[6], (right, above)),
        remote(pack.at[0], g_c.at[1], s_h.at[7], r_h.at[7], (left, above)),
        remote(pack.at[1], g_c.at[2], s_h.at[8], r_h.at[8], (right, below)),
        remote(pack.at[0], g_c.at[3], s_h.at[9], r_h.at[9], (left, below)),
    ]
    for copy in halos:
        copy.start()

    b_a[gx] = packed

    @pl.loop(1, nx)
    def _(o):
        src = lax.rem(gx + o, nx)
        remote(tile, b_a.at[src], s_a.at[0], r_a.at[src], (gx, gy)).wait_recv()

    wave = lax.dot_general(
        b_a[...].reshape(nx * 8, 128), q_mat[...], (((1,), (1,)), ((), ())),
        precision=HIGHEST, preferred_element_type=F32,
    )
    real = jnp.zeros((8, 128), F32)
    imag = jnp.zeros((8, 128), F32)
    for g in range(nx):
        t_re, t_im = wave[8 * g : 8 * g + 8, 0:128], wave[8 * g : 8 * g + 8, 128:256]
        c, s = twist[0, g : g + 1, :], twist[1, g : g + 1, :]
        real = real + (t_re * c + t_im * s)
        imag = imag + (t_im * c - t_re * s)

    lane8 = iota((8, 128), 1)
    is_y = (lane8 >= 32) & (lane8 < 64)
    flip = jnp.where(is_y, np.float32(-1), np.float32(1))
    dn[0] = real * flip
    dn[1] = imag * flip
    for r in range(8):
        up[0, r : r + 1, :] = real[7 - r : 8 - r]
        up[1, r : r + 1, :] = imag[7 - r : 8 - r]

    @pl.loop(1, ny)
    def _(o):
        to = gy + o

        @pl.when(to < ny)
        def _():
            remote(up, b_b.at[gy], s_b.at[o], r_b.at[gy], (gx, to)).start()

        @pl.when(to >= ny)
        def _():
            remote(dn, b_b.at[gy], s_b.at[o], r_b.at[gy], (gx, to - ny)).start()

    zero = jnp.zeros((8, 128), F32)

    def swapped(s):
        return jnp.where(lane8 < 32, pltpu.roll(s, 96, 1), pltpu.roll(s, 32, 1))

    def add_source(d, parts, acc):
        acc = list(acc)
        for p in range(2):
            s = parts[p]
            t = swapped(s)
            for w in range(WINDOWS):
                rows = pl.ds(8 * d + w, 8)
                acc[2 * w + p] = acc[2 * w + p] + tab[p, rows, :] * s + tab2[p, rows, :] * t
        acc[-1] = acc[-1] + parts[1]
        return tuple(acc)

    def arrive(src):
        remote(up, b_b.at[src], s_b.at[0], r_b.at[src], (gx, gy)).wait_recv()
        return b_b[src, 0], b_b[src, 1]

    start = tuple(zero for _ in range(2 * WINDOWS + 1))
    acc_up = add_source(0, (up[0], up[1]), start)
    acc_up = lax.fori_loop(1, gy + 1, lambda d, a: add_source(d, arrive(gy - d), a), acc_up)
    acc_dn = lax.fori_loop(1, ny - gy, lambda d, a: add_source(d, arrive(gy + d), a), start)

    alternate = jnp.where(iota((8, 128), 0) % 2 == 0, np.float32(1), np.float32(-1))
    last = jnp.sum((flip * acc_dn[-1] - acc_up[-1]) * alternate, axis=0, keepdims=True)
    last = jnp.broadcast_to(last, (8, 128))
    last = swapped(last)
    last = jnp.where(((lane8 == 0) | (lane8 == 32)) & (gx == 0), last, 0.0) * np.float32(corner)

    row16 = iota((16, 128), 0)
    field = []
    for p in range(2):
        out = jnp.zeros((16, 128), F32)
        for w in range(WINDOWS):
            sums = acc_up[2 * w + p] + flip * acc_dn[2 * (WINDOWS - 1 - w) + p]
            if p == 1:
                sign = np.float32((1 if w % 2 else -1) / 8)
                sums = sums + sign * last
            line = jnp.sum(sums, axis=0, keepdims=True)
            out = jnp.where(row16 == w, jnp.broadcast_to(line, (16, 128)), out)
        field.append(out)

    turned = []
    for g in range(nx):
        c, s = twist[0, g : g + 1, :], twist[1, g : g + 1, :]
        turned.append(
            jnp.concatenate([field[0] * c - field[1] * s, field[0] * s + field[1] * c], axis=1)
        )
    turned = jnp.concatenate(turned, axis=0)
    shares = jnp.dot(turned, q_mat[...], precision=HIGHEST, preferred_element_type=F32)
    send_c[...] = shares.reshape(nx, 16, 128)

    @pl.loop(1, nx)
    def _(o):
        to = lax.rem(gx + o, nx)
        remote(send_c.at[to], b_c.at[gx], s_c.at[o], r_c.at[gx], (to, gy)).start()

    b_c[gx] = send_c[gx]
    for copy in halos:
        copy.wait_recv()
    hy_ang[...] = g_ang[...]
    hy_spc[...] = g_spc[...]
    hx[...] = g_x[...]
    hc[...] = g_c[...]

    @pl.loop(1, nx)
    def _(o):
        src = lax.rem(gx + o, nx)
        remote(send_c.at[0], b_c.at[src], s_c.at[0], r_c.at[src], (gx, gy)).wait_recv()

    whole = b_c[0]
    for g in range(1, nx):
        whole = whole + b_c[g]
    fld[...] = whole

    for copy in halos:
        copy.wait_send()

    @pl.loop(1, nx)
    def _(o):
        remote(tile, b_a.at[0], s_a.at[o], r_a.at[0], (gx, gy)).wait_send()
        remote(send_c.at[0], b_c.at[0], s_c.at[o], r_c.at[0], (gx, gy)).wait_send()

    @pl.loop(1, ny)
    def _(o):
        remote(up, b_b.at[0], s_b.at[o], r_b.at[0], (gx, gy)).wait_send()


def cross(a, b):
    return (
        a[1] * b[2] - a[2] * b[1],
        a[2] * b[0] - a[0] * b[2],
        a[0] * b[1] - a[1] * b[0],
    )


def torque(v, h):
    p = cross(v, h)
    r = cross(v, p)
    return [
        (a + np.float32(DAMPING) * b) * np.float32(-1.0 / (1.0 + DAMPING * DAMPING))
        for a, b in zip(p, r)
    ]


def normalized(w):
    s = w[0] * w[0] + w[1] * w[1] + w[2] * w[2]
    r = lax.rsqrt(s)
    r = r * (1.5 - 0.5 * s * r * r)
    return [c * r for c in w]


def heun_kernel(
    nx, ny,
    ang, spc, fld, hy_ang, hy_spc, hx, hc, lanes,
    nxt, dip,
    raw, cpl, vec, wgt, dpl,
):
    gx, gy = lax.axis_index("gx"), lax.axis_index("gy")
    for c in range(3):
        dip[c, 0] = fld[1:9, 32 * c : 32 * c + 32]

    comp = iota((128, 256), 0)
    atom = iota((128, 256), 1)
    want = jnp.where(atom < 128, atom >> 2, jnp.where(atom < 192, 97, 96))
    scale = jnp.where(atom < 128, 32, 2)
    row8 = iota((8, 256), 0)
    for c in range(3):
        hot = jnp.where(comp == want + scale * c, np.float32(1), np.float32(0))
        lines = jnp.dot(fld[...], hot, precision=HIGHEST, preferred_element_type=F32)

        def line(w):
            return jnp.broadcast_to(lines[w : w + 1], (8, 256))

        for t in range(4):
            dpl[c, pl.ds(8 * t, 8), :] = jnp.where(row8 < 4, line(2 * t + 1), line(2 * t + 2))
        dpl[c, pl.ds(32, 8), :] = jnp.where(row8 < 4, line(9), line(0))

    cols = jnp.concatenate(
        [hx[0], hx[1], hc[0], hc[1], hc[2], hc[3], jnp.zeros((80, 128), F32)], axis=0
    )
    cols = jnp.transpose(cols)
    lane32 = iota((32, 128), 1)
    lane8, rowh = iota((8, 128), 1), iota((8, 128), 0)

    for q in range(3):
        for sub in range(2):
            n = 2 * q + sub
            for z in range(4):

                def column(piece):
                    part = cols[32 * z : 32 * z + 32, 8 * piece + n : 8 * piece + n + 1]
                    return jnp.broadcast_to(part, (32, 128))

                def spot(piece, y):
                    part = cols[32 * z + y : 32 * z + y + 1, 8 * piece + n : 8 * piece + n + 1]
                    return jnp.broadcast_to(part, (8, 128))

                def edge(side):
                    if q < 2:
                        return jnp.broadcast_to(hy_ang[sub, q, z, side : side + 1, :], (8, 128))
                    return jnp.broadcast_to(hy_spc[sub, z, side : side + 1, :], (8, 128)).astype(F32)

                raw[n, z, 0:32, 0:128] = ang[sub, q, z] if q < 2 else spc[sub, z].astype(F32)
                raw[n, z, 0:32, 128:256] = jnp.where(lane32 < 64, column(1), column(0))
                raw[n, z, 32:40, 0:128] = jnp.where(rowh < 4, edge(1), edge(0))
                low = jnp.where(lane8 < 64, spot(3, 31), spot(2, 31))
                high = jnp.where(lane8 < 64, spot(5, 0), spot(4, 0))
                raw[n, z, 32:40, 128:256] = jnp.where(rowh < 4, high, low)

    row = iota((40, 256), 0)
    col = iota((40, 256), 1)
    y = gy * 32 + jnp.where(row < 36, row, row - 40)
    x = gx * 128 + jnp.where(col < 192, col, col - 256)
    inside = (y >= 0) & (y < ny * 32) & (x >= 0) & (x < nx * 128)

    for sub in range(2):
        for z in range(4):
            cobalt = raw[4 + sub, z] > 0.5
            coupling = jnp.where(inside, pick(cobalt, COUPLING_PAIR), 0.0)
            cpl[sub, z] = coupling
            v = unit(raw[sub, z], raw[2 + sub, z])
            for c in range(3):
                vec[sub, c, z] = v[c]
                wgt[sub, c, z] = coupling * v[c]

    def neighbours(sub, c, z):
        other = 1 - sub
        near = wgt[other, c, z]
        far = z - 1 if sub == 0 else z + 1
        if 0 <= far < 4:
            near = near + wgt[other, c, far]
        near = near + pltpu.roll(near, 1 if sub == 0 else 255, 1)
        return near + pltpu.roll(near, 1 if sub == 0 else 39, 0)

    def total_field(sub, z, v, n, cobalt, d):
        ratio = pick(cobalt, [np.float32(EXCHANGE_SCALE) * np.float32(r) for r in RATIO_PAIR])
        h = [ratio * n[c] + d[c] for c in range(3)]
        h[2] = h[2] + pick(cobalt, EASY_PAIR) * v[2]
        return h

    ahead = {}
    for sub in range(2):
        for z in range(4):
            cobalt = raw[4 + sub, z] > 0.5
            v = [vec[sub, c, z] for c in range(3)]
            n = [neighbours(sub, c, z) for c in range(3)]
            f = torque(v, total_field(sub, z, v, n, cobalt, [dpl[c] for c in range(3)]))
            p = normalized([a + np.float32(TIME_STEP) * b for a, b in zip(v, f)])
            for c in range(3):
                raw[3 * sub + c, z] = p[c]
                nxt[sub, c, z] = f[c][0:32, 0:128]
    for sub in range(2):
        for z in range(4):
            for c in range(3):
                wgt[sub, c, z] = cpl[sub, z] * raw[3 * sub + c, z]
    for sub in range(2):
        for z in range(4):
            cobalt = spc[sub, z] == 1
            p = [raw[3 * sub + c, z, 0:32, 0:128] for c in range(3)]
            n = [neighbours(sub, c, z)[0:32, 0:128] for c in range(3)]
            d = [dpl[c, 0:32, 0:128] for c in range(3)]
            f = torque(p, total_field(sub, z, p, n, cobalt, d))
            w = [
                vec[sub, c, z, 0:32, 0:128] + np.float32(0.5 * TIME_STEP) * (nxt[sub, c, z] + f[c])
                for c in range(3)
            ]
            w = normalized(w)
            for c in range(3):
                nxt[sub, c, z] = w[c]


def solution(mesh):
    nx, ny = mesh.shape["gx"], mesh.shape["gy"]
    table, corner = wave_tables(nx, ny)
    base, phase, twist, lanes = trig_tables(nx)
    vmem = pl.BlockSpec(memory_space=pltpu.VMEM)
    dma = pltpu.SemaphoreType.DMA

    def scratch(*shape, dtype=F32):
        return pltpu.VMEM(shape, dtype)

    def on_device(spin_angles, species):
        halves = pl.pallas_call(
            functools.partial(gather_kernel, nx, ny, corner),
            out_shape=[
                jax.ShapeDtypeStruct((16, 128), F32),
                jax.ShapeDtypeStruct((2, 2, 4, 2, 128), F32),
                jax.ShapeDtypeStruct((2, 4, 2, 128), jnp.int32),
                jax.ShapeDtypeStruct((2, 8, 128), F32),
                jax.ShapeDtypeStruct((4, 8, 128), F32),
            ],
            in_specs=[vmem, vmem, pl.BlockSpec(memory_space=pl.ANY), vmem, vmem, vmem, vmem],
            out_specs=[vmem] * 5,
            scratch_shapes=[
                scratch(3, 32, 128),
                scratch(8, 128),
                scratch(nx, 8, 128),
                scratch(256, 128),
                scratch(2, TABLE_ROWS, 128),
                scratch(2, TABLE_ROWS, 128),
                scratch(2, 8, 128),
                scratch(2, 8, 128),
                scratch(ny, 2, 8, 128),
                scratch(nx, 16, 128),
                scratch(nx, 16, 128),
                scratch(2, 8, 128),
                scratch(2, 2, 4, 2, 128),
                scratch(2, 4, 2, 128, dtype=jnp.int32),
                scratch(2, 8, 128),
                scratch(4, 8, 128),
                dma((2,)),
                dma((nx,)),
                dma((nx,)),
                dma((ny,)),
                dma((ny,)),
                dma((nx,)),
                dma((nx,)),
                dma((10,)),
                dma((10,)),
            ],
            compiler_params=pltpu.CompilerParams(collective_id=0, has_side_effects=True),
        )(spin_angles, species, table, base, phase, twist, lanes)
        fld, hy_ang, hy_spc, hx, hc = halves
        return pl.pallas_call(
            functools.partial(heun_kernel, nx, ny),
            out_shape=[
                jax.ShapeDtypeStruct((2, 3, 4, 32, 128), F32),
                jax.ShapeDtypeStruct((3, 1, 8, 32), F32),
            ],
            in_specs=[vmem] * 8,
            out_specs=[vmem] * 2,
            scratch_shapes=[
                scratch(6, 4, 40, 256),
                scratch(2, 4, 40, 256),
                scratch(2, 3, 4, 40, 256),
                scratch(2, 3, 4, 40, 256),
                scratch(3, 40, 256),
            ],
        )(spin_angles, species, fld, hy_ang, hy_spc, hx, hc, lanes)

    return jax.shard_map(
        lambda a, s: tuple(on_device(a, s)),
        mesh=mesh,
        in_specs=(P(None, None, None, "gy", "gx"), P(None, None, "gy", "gx")),
        out_specs=(P(None, None, None, "gy", "gx"), P(None, None, "gy", "gx")),
        check_vma=False,
    )
```

```python
import functools
import math

import jax
import jax.numpy as jnp
import numpy as np
from jax import lax
from jax.experimental import pallas as pl
from jax.experimental.pallas import tpu as pltpu
from jax.sharding import PartitionSpec as P

MESH = pl.DeviceIdType.MESH
F32, BF16 = jnp.float32, jnp.bfloat16

CELLS_M = 4
DAMPING = 0.1
TIME_STEP = 0.05
EXCHANGE_SCALE = 0.6
DIPOLE = 2.0
MOMENT_PAIR = (2.22, 1.72)
COUPLING_PAIR = (1.0, 1.25)
ANISOTROPY_PAIR = (0.3, 0.9)
RATIO_PAIR = (COUPLING_PAIR[0] / MOMENT_PAIR[0], COUPLING_PAIR[1] / MOMENT_PAIR[1])
EASY_PAIR = (2 * ANISOTROPY_PAIR[0] / MOMENT_PAIR[0], 2 * ANISOTROPY_PAIR[1] / MOMENT_PAIR[1])

PART_K = 32
ROWS = 8
COLS = 32
WINDOWS = 10
TABLE_LEAD = 8
TABLE_ROWS = 400


def wave_tables(nx, ny):
    period_x, period_y = 2 * nx * COLS, 2 * ny * ROWS
    half_y = period_y // 2
    v = np.arange(period_x // 2 + 1)
    u = np.arange(half_y + 1)
    a = 2 * np.pi * v[:, None] / period_x
    b = 2 * np.pi * u[None, :] / period_y
    k = np.sqrt(a * a + b * b)
    inv = np.where(k > 0, 1.0 / np.where(k > 0, k, 1.0), 0.0)
    g = {
        "xx": -a * a * 0.5 * inv,
        "yy": -b * b * 0.5 * inv,
        "zz": 0.5 * k - 1.0,
        "xy": -a * b * 0.5 * inv,
    }
    dy = np.arange(-TABLE_LEAD, TABLE_ROWS - TABLE_LEAD)
    angle = 2 * np.pi * ((u[:, None] * dy[None, :]) % period_y) / period_y
    fold = np.where((u == 0) | (u == half_y), 1.0, 2.0)
    cosine = fold[:, None] * np.cos(angle)
    sine = np.where((u == 0) | (u == half_y), 0.0, 2.0)[:, None] * np.sin(angle)
    scale = DIPOLE / (period_x * period_y) * np.where((v == 0) | (v == period_x // 2), 1.0, 2.0)
    tables = [scale[:, None] * (g[n] @ cosine) for n in ("xx", "yy", "zz")]
    odd = scale[:, None] * (g["xy"] @ sine)
    odd[-1] = 0.0
    tables.append(odd)
    lanes = np.stack(tables)
    out = np.zeros((nx + 1, TABLE_ROWS, 4 * PART_K), np.float32)
    for s in range(nx):
        block = lanes[:, s * PART_K : (s + 1) * PART_K, :]
        out[s] = block.transpose(2, 0, 1).reshape(TABLE_ROWS, -1)
    out[nx] = out[0]
    for n in range(4):
        out[nx, :, n * PART_K] = lanes[n, -1, :]
    corner = DIPOLE / (period_x * period_y) * float(-0.5 * np.pi * np.pi / np.sqrt(2 * np.pi**2))
    return out, corner


def trig_tables(nx):
    period = 2 * nx * COLS
    lane = np.arange(128)
    comp = np.where(lane < 96, lane // 32, np.where(lane < 102, (lane - 96) // 2, 3))
    place = np.where(lane < 96, lane % 32, np.where(lane % 2 == 0, -1, 32))
    j = np.arange(PART_K)
    t = 2 * np.pi * ((j[:, None] * place[None, :]) % period) / period
    base = np.stack([np.cos(t), np.sin(t)]).astype(np.float32)
    s = np.arange(nx)
    t = 2 * np.pi * ((s[:, None] * PART_K * place[None, :]) % period) / period
    phase = np.stack([np.cos(t), np.sin(t)], axis=1).astype(np.float32)
    jl = lane % 32
    t = 2 * np.pi * ((s[:, None] * COLS * jl[None, :]) % period) / period
    twist = np.stack([np.cos(t), np.sin(t)]).astype(np.float32)
    row = np.stack([comp, np.where(place % 2 == 0, 1, -1)]).astype(np.float32)
    return base, phase, twist, row


def sine(r):
    q = r * r
    p = 1.0 / 6227020800.0
    for c in (-1.0 / 39916800.0, 1.0 / 362880.0, -1.0 / 5040.0, 1.0 / 120.0, -1.0 / 6.0):
        p = p * q + c
    return r + r * q * p


def sine_cosine(x):
    size = jnp.abs(x)
    far = (np.float32(math.pi) - size) + np.float32(math.pi - float(np.float32(math.pi)))
    s = sine(jnp.where(size > np.float32(math.pi / 2), far, size))
    half = (np.float32(math.pi / 2) - size) + np.float32(
        math.pi / 2 - float(np.float32(math.pi / 2))
    )
    return jnp.where(x < 0, -s, s), sine(half)


def pick(cobalt, pair):
    return jnp.where(cobalt, np.float32(pair[1]), np.float32(pair[0]))


def unit(polar, azimuth):
    sp, cp = sine_cosine(polar)
    sq, cq = sine_cosine(azimuth)
    return sp * cq, sp * sq, cp


def iota(shape, dim):
    return lax.broadcasted_iota(jnp.int32, shape, dim)


def cross(a, b):
    return (
        a[1] * b[2] - a[2] * b[1],
        a[2] * b[0] - a[0] * b[2],
        a[0] * b[1] - a[1] * b[0],
    )


def torque(v, h):
    p = cross(v, h)
    r = cross(v, p)
    return [
        (a + np.float32(DAMPING) * b) * np.float32(-1.0 / (1.0 + DAMPING * DAMPING))
        for a, b in zip(p, r)
    ]


def normalized(w):
    s = w[0] * w[0] + w[1] * w[1] + w[2] * w[2]
    r = lax.rsqrt(s)
    r = r * (1.5 - 0.5 * s * r * r)
    return [c * r for c in w]


def split(x, pieces):
    out = []
    for _ in range(pieces):
        out.append(x.astype(BF16))
        x = x - out[-1].astype(F32)
    return out


def dot(a, b, dims=(1, 0)):
    return lax.dot_general(
        a, b, (((dims[0],), (dims[1],)), ((), ())), preferred_element_type=F32
    )


def exact_dot(a, hot):
    n = a.shape[0]
    out = dot(jnp.concatenate(split(a, 3), axis=0), hot)
    return out[0:n] + out[n : 2 * n] + out[2 * n : 3 * n]


def wide_dot(a, b_high, b_low, dims):
    n = a.shape[0]
    high, low = split(a, 2)
    out = dot(jnp.concatenate([high, low], axis=0), b_high, dims)
    return out[0:n] + out[n : 2 * n] + dot(high, b_low, dims)


def step_kernel(
    nx, ny, corner,
    ang_hbm, spc_hbm, table_hbm, base, phase, twist, lanes,
    nxt, dip,
    ang, spc, mom, tile, b_a, q_high, q_low, tab, tab2, up, dn, b_b, send_c, b_c, pack, g_ang, g_spc, g_x, g_c,
    raw, cpl, vec, wgt, fix, dpl,
    load_sem, s_a, r_a, s_b, r_b, s_f, r_f, s_c, r_c, s_h, r_h, rise, fall,
):
    gx, gy = lax.axis_index("gx"), lax.axis_index("gy")
    left, right = lax.rem(gx + nx - 1, nx), lax.rem(gx + 1, nx)
    below, above = lax.rem(gy + ny - 1, ny), lax.rem(gy + 1, ny)
    core = lax.rem(gy, 2)
    chip = gy // 2
    partner = gy + 1 - 2 * core
    chips = ny // 2
    half = ny // 2
    row = lax.rem(gy, half)
    z_up = gy - row + lax.rem(row + 2, half)
    z_down = gy - row + lax.rem(row + half - 2, half)
    opposite = lax.rem(gy + half, ny)

    loads = []
    for sub in range(2):
        loads.append(pltpu.make_async_copy(ang_hbm.at[sub], ang.at[sub], load_sem.at[2 * sub]))
        loads.append(pltpu.make_async_copy(spc_hbm.at[sub], spc.at[sub], load_sem.at[2 * sub + 1]))
    late_loads = [
        pltpu.make_async_copy(table_hbm.at[gx], tab.at[0], load_sem.at[4]),
        pltpu.make_async_copy(table_hbm.at[jnp.where(gx == 0, nx, gx)], tab.at[1], load_sem.at[5]),
    ]
    for load in loads + late_loads:
        load.start()

    barrier = pltpu.get_barrier_semaphore()

    def signal(semaphore, device):
        pl.semaphore_signal(semaphore, inc=1, device_id=device, device_id_type=MESH)

    @pl.loop(1, nx)
    def _(o):
        signal(barrier, (lax.rem(gx + o, nx), gy))

    for other in (above, below, z_up, z_down, opposite):
        signal(barrier, (gx, other))

    def remote(src, dst, send, recv, device):
        return pltpu.make_async_remote_copy(
            src_ref=src, dst_ref=dst, send_sem=send, recv_sem=recv, device_id=device, device_id_type=MESH
        )

    total = [jnp.zeros((32, 128), F32) for _ in range(3)]
    for sub in range(2):
        loads[2 * sub].wait()
        loads[2 * sub + 1].wait()
        for z in range(4):
            moment = pick(spc[sub, z] == 1, MOMENT_PAIR)
            v = unit(ang[sub, 0, z], ang[sub, 1, z])
            for c in range(3):
                vec[sub, c, z, 0:32, 0:128] = v[c]
            total = [t + moment * c for t, c in zip(total, v)]
    rows = []
    for c in range(3):
        mom[c] = total[c]
        line = mom[c, pl.ds(0, 8, 4), :]
        for r in range(1, 4):
            line = line + mom[c, pl.ds(r, 8, 4), :]
        rows.append(line)
    atom = iota((384, 128), 0)
    place = ((atom >> 7) << 5) + ((atom & 127) >> 2)
    spread = jnp.where(iota((384, 128), 1) == place, 1 / 128, 0.0).astype(BF16)
    packed = exact_dot(jnp.concatenate(rows, axis=1), spread)
    tile[...] = packed

    pl.semaphore_wait(barrier, nx - 1 + 5)

    @pl.loop(1, nx)
    def _(o):
        remote(tile, b_a.at[gx], s_a, r_a, (lax.rem(gx + o, nx), gy)).start()

    def tell(t):
        signal(rise.at[t], (gx, z_up))
        signal(fall.at[t], (gx, z_down))

    def hear(t):
        pl.semaphore_wait(rise.at[t], 1)
        pl.semaphore_wait(fall.at[t], 1)

    hops = half // 4
    halo_row, halo_spc, halo_x, halo_c = [
        [remote(src, dst, s_h.at[n], r_h.at[n], to) for src, dst, to in pair]
        for n, pair in enumerate((
            ((ang.at[:, :, :, pl.ds(31, 1), :], g_ang.at[:, :, :, pl.ds(0, 1), :], (gx, above)),
             (ang.at[:, :, :, pl.ds(0, 1), :], g_ang.at[:, :, :, pl.ds(1, 1), :], (gx, below))),
            ((spc.at[:, :, pl.ds(31, 1), :], g_spc.at[:, :, pl.ds(0, 1), :], (gx, above)),
             (spc.at[:, :, pl.ds(0, 1), :], g_spc.at[:, :, pl.ds(1, 1), :], (gx, below))),
            ((pack.at[1], g_x.at[0], (right, gy)), (pack.at[0], g_x.at[1], (left, gy))),
            ((g_x, g_c.at[0], (gx, above)), (g_x, g_c.at[1], (gx, below))),
        ))
    ]
    halo_all = [remote(g, g, s_h.at[n], r_h.at[n], (gx, gy)) for n, g in enumerate((g_ang, g_spc, g_x, g_c))]

    tell(0)
    b_a[gx] = packed

    lane = iota((128, 128), 1)
    edges = jnp.zeros((128, 128), F32)
    for q in range(3):
        for sub in range(2):
            n = 2 * q + sub
            block = ang[sub, q] if q < 2 else spc[sub].astype(F32)
            block = block.reshape(128, 128)
            edges = jnp.where(lane == n, pltpu.roll(block, n, 1) if n else block, edges)
            edges = jnp.where(lane == 8 + n, pltpu.roll(block, n + 9, 1), edges)
    edges = jnp.transpose(edges)
    pack[0] = edges[0:8]
    pack[1] = edges[8:16]
    for copy in halo_x + halo_row + halo_spc:
        copy.start()
    hear(0)
    tell(1)

    b_cos, b_sin = base[0], base[1]
    p_cos, p_sin = phase[gx, 0:1, :], phase[gx, 1:2, :]
    cosine = b_cos * p_cos - b_sin * p_sin
    sinus = b_sin * p_cos + b_cos * p_sin
    comp, parity = lanes[0:1, :], lanes[1:2, :]
    single = (iota((32, 128), 0) + gx) == 0

    def store_q(at, q):
        q_high[pl.ds(at, 32), :], q_low[pl.ds(at, 32), :] = split(q, 2)

    for c in range(3):
        mine = comp == np.float32(c)
        real, imag = (sinus, cosine) if c == 1 else (cosine, -sinus)
        store_q(32 * c, jnp.where(mine, jnp.where(single, 1.0, real), 0.0))
        store_q(128 + 32 * c, jnp.where(mine, jnp.where(single, parity, imag), 0.0))
    store_q(96, jnp.zeros((32, 128), F32))
    store_q(224, jnp.zeros((32, 128), F32))
    hear(1)
    tell(2)

    for load in late_loads:
        load.wait()
    wide = iota((TABLE_ROWS, 128), 1)
    for p in range(2):
        t = tab[p]
        tab2[p] = jnp.where(
            wide < 32,
            pltpu.roll(t, 32, 1),
            jnp.where(wide < 64, -pltpu.roll(t, 64, 1), 0.0),
        )
        hear(2 + p)
        tell(3 + p)
    for t in range(4, hops):
        hear(t)
        if t + 1 < hops:
            tell(t + 1)

    def blocks(ref, n, send, recv):
        return remote(ref.at[pl.ds(0, n)], ref.at[pl.ds(0, n)], send, recv, (gx, gy))

    blocks(b_a, nx - 1, s_a, r_a).wait_recv()

    wave = wide_dot(b_a[...].reshape(nx * 8, 128), q_high[...], q_low[...], (1, 1))
    real = jnp.zeros((8, 128), F32)
    imag = jnp.zeros((8, 128), F32)
    for g in range(nx):
        t_re, t_im = wave[8 * g : 8 * g + 8, 0:128], wave[8 * g : 8 * g + 8, 128:256]
        c, s = twist[0, g : g + 1, :], twist[1, g : g + 1, :]
        real = real + (t_re * c + t_im * s)
        imag = imag + (t_im * c - t_re * s)

    lane8 = iota((8, 128), 1)
    is_y = (lane8 >= 32) & (lane8 < 64)
    flip = jnp.where(is_y, np.float32(-1), np.float32(1))
    dn[0] = real * flip
    dn[1] = imag * flip
    for r in range(8):
        up[0, r : r + 1, :] = real[7 - r : 8 - r]
        up[1, r : r + 1, :] = imag[7 - r : 8 - r]

    @pl.loop(1, chips)
    def _(k):
        to = lax.rem(gy + 2 * k, ny)

        @pl.when(to > gy)
        def _():
            remote(up, b_b.at[core, chip], s_b, r_b, (gx, to)).start()

        @pl.when(to < gy)
        def _():
            remote(dn, b_b.at[core, chip], s_b, r_b, (gx, to)).start()

    even = core == 0
    b_b[core, chip] = jnp.where(even, up[...], dn[...])

    halo_all[2].wait_recv()
    for copy in halo_c:
        copy.start()
    halo_all[0].wait_recv()
    halo_all[1].wait_recv()
    halo_all[3].wait_recv()

    cols = jnp.concatenate(
        [g_x[0], g_x[1], g_c[0, 0], g_c[0, 1], g_c[1, 0], g_c[1, 1], jnp.zeros((80, 128), F32)], axis=0
    )
    cols = jnp.transpose(cols)
    lane32 = iota((32, 128), 1)
    rowh = iota((8, 128), 0)
    for q in range(3):
        for sub in range(2):
            n = 2 * q + sub
            for z in range(4):

                def column(piece):
                    part = cols[32 * z : 32 * z + 32, 8 * piece + n : 8 * piece + n + 1]
                    return jnp.broadcast_to(part, (32, 128))

                def spot(piece, y):
                    part = cols[32 * z + y : 32 * z + y + 1, 8 * piece + n : 8 * piece + n + 1]
                    return jnp.broadcast_to(part, (8, 128))

                def edge(side):
                    if q < 2:
                        return jnp.broadcast_to(g_ang[sub, q, z, side : side + 1, :], (8, 128))
                    return jnp.broadcast_to(g_spc[sub, z, side : side + 1, :], (8, 128)).astype(F32)

                if q == 2:
                    raw[n, z, 0:32, 0:128] = spc[sub, z].astype(F32)
                raw[n, z, 0:32, 128:256] = jnp.where(lane32 < 64, column(1), column(0))
                raw[n, z, 32:40, 0:128] = jnp.where(rowh < 4, edge(1), edge(0))
                low = jnp.where(lane8 < 64, spot(3, 31), spot(2, 31))
                high = jnp.where(lane8 < 64, spot(5, 0), spot(4, 0))
                raw[n, z, 32:40, 128:256] = jnp.where(rowh < 4, high, low)

    at_row = iota((40, 256), 0)
    at_col = iota((40, 256), 1)
    y = gy * 32 + jnp.where(at_row < 36, at_row, at_row - 40)
    x = gx * 128 + jnp.where(at_col < 192, at_col, at_col - 256)
    inside = (y >= 0) & (y < ny * 32) & (x >= 0) & (x < nx * 128)
    for sub in range(2):
        for z in range(4):
            for r, l in ((slice(0, 32), slice(128, 256)), (slice(32, 40), slice(0, 256))):
                v = unit(raw[sub, z, r, l], raw[2 + sub, z, r, l])
                for c in range(3):
                    vec[sub, c, z, r, l] = v[c]
            coupling = jnp.where(inside, pick(raw[4 + sub, z] > 0.5, COUPLING_PAIR), 0.0)
            cpl[sub, z] = coupling
            for c in range(3):
                wgt[sub, c, z] = coupling * vec[sub, c, z]

    def neighbours(sub, c, z):
        other = 1 - sub
        near = wgt[other, c, z]
        far = z - 1 if sub == 0 else z + 1
        if 0 <= far < 4:
            near = near + wgt[other, c, far]
        near = near + pltpu.roll(near, 1 if sub == 0 else 255, 1)
        return near + pltpu.roll(near, 1 if sub == 0 else 39, 0)

    ratio_pair = [np.float32(EXCHANGE_SCALE) * np.float32(r) for r in RATIO_PAIR]
    for sub in range(2):
        for z in range(4):
            cobalt = raw[4 + sub, z] > 0.5
            ratio = pick(cobalt, ratio_pair)
            for c in range(3):
                h = ratio * neighbours(sub, c, z)
                if c == 2:
                    h = h + pick(cobalt, EASY_PAIR) * vec[sub, c, z]
                fix[sub, c, z] = h

    blocks(b_b.at[core], chips - 1, s_b, r_b).wait_recv()
    hand_on = remote(b_b.at[core], b_b.at[core], s_f, r_f, (gx, partner))
    hand_on.start()

    zero = jnp.zeros((8, 128), F32)

    def swapped(s):
        return jnp.where(lane8 < 32, pltpu.roll(s, 96, 1), pltpu.roll(s, 32, 1))

    def add_source(d, parts, acc):
        acc = list(acc)
        for p in range(2):
            s = parts[p]
            t = swapped(s)
            for w in range(WINDOWS):
                span = pl.ds(8 * d + w, 8)
                acc[2 * w + p] = acc[2 * w + p] + tab[p, span, :] * s + tab2[p, span, :] * t
        acc[-1] = acc[-1] + parts[1]
        return tuple(acc)

    def add_chips(which, acc_up, acc_dn):
        def source(k):
            return b_b[which, k, 0], b_b[which, k, 1]

        acc_up = lax.fori_loop(
            0, chip, lambda k, a: add_source(gy - (2 * k + which), source(k), a), acc_up
        )
        acc_dn = lax.fori_loop(
            chip + 1, chips, lambda k, a: add_source(2 * k + which - gy, source(k), a), acc_dn
        )
        return acc_up, acc_dn

    start = tuple(zero for _ in range(2 * WINDOWS + 1))
    acc_up = add_source(0, (up[0], up[1]), start)
    acc_up, acc_dn = add_chips(core, acc_up, start)
    blocks(b_b.at[1 - core], chips, s_f, r_f).wait_recv()
    acc_up, acc_dn = add_chips(1 - core, acc_up, acc_dn)
    beside = (b_b[1 - core, chip, 0], b_b[1 - core, chip, 1])
    acc_up = lax.fori_loop(0, core, lambda _, a: add_source(1, beside, a), acc_up)
    acc_dn = lax.fori_loop(0, 1 - core, lambda _, a: add_source(1, beside, a), acc_dn)

    alternate = jnp.where(iota((8, 128), 0) % 2 == 0, np.float32(1), np.float32(-1))
    last = jnp.sum((flip * acc_dn[-1] - acc_up[-1]) * alternate, axis=0, keepdims=True)
    last = jnp.broadcast_to(last, (8, 128))
    last = swapped(last)
    last = jnp.where(((lane8 == 0) | (lane8 == 32)) & (gx == 0), last, 0.0) * np.float32(corner)

    row16 = iota((16, 128), 0)
    field = []
    for p in range(2):
        out = jnp.zeros((16, 128), F32)
        for w in range(WINDOWS):
            sums = acc_up[2 * w + p] + flip * acc_dn[2 * (WINDOWS - 1 - w) + p]
            if p == 1:
                sign = np.float32((1 if w % 2 else -1) / 8)
                sums = sums + sign * last
            line = jnp.sum(sums, axis=0, keepdims=True)
            out = jnp.where(row16 == w, jnp.broadcast_to(line, (16, 128)), out)
        field.append(out)

    turned = []
    for g in range(nx):
        c, s = twist[0, g : g + 1, :], twist[1, g : g + 1, :]
        turned.append(
            jnp.concatenate([field[0] * c - field[1] * s, field[0] * s + field[1] * c], axis=1)
        )
    shares = wide_dot(jnp.concatenate(turned, axis=0), q_high[...], q_low[...], (1, 0))
    send_c[...] = shares.reshape(nx, 16, 128)

    @pl.loop(1, nx)
    def _(o):
        to = lax.rem(gx + o, nx)
        remote(send_c.at[to], b_c.at[gx], s_c, r_c, (to, gy)).start()

    b_c[gx] = send_c[gx]
    atom = iota((128, 256), 1)
    want = jnp.where(atom < 128, atom >> 2, jnp.where(atom < 192, 97, 96))
    scale = jnp.where(atom < 128, 32, 2)
    hot = [
        jnp.where(iota((128, 256), 0) == want + scale * c, 1.0, 0.0).astype(BF16) for c in range(3)
    ]
    row8 = iota((8, 256), 0)

    blocks(b_c, nx - 1, s_c, r_c).wait_recv()
    whole = b_c[0]
    for g in range(1, nx):
        whole = whole + b_c[g]

    for c in range(3):
        dip[c, 0] = whole[1:9, 32 * c : 32 * c + 32]
        lines = exact_dot(whole, hot[c])

        def line(w):
            return jnp.broadcast_to(lines[w : w + 1], (8, 256))

        for t in range(4):
            dpl[c, pl.ds(8 * t, 8), :] = jnp.where(row8 < 4, line(2 * t + 1), line(2 * t + 2))
        dpl[c, pl.ds(32, 8), :] = jnp.where(row8 < 4, line(9), line(0))

    for sub in range(2):
        for z in range(4):
            v = [vec[sub, c, z] for c in range(3)]
            f = torque(v, [fix[sub, c, z] + dpl[c] for c in range(3)])
            p = normalized([a + np.float32(TIME_STEP) * b for a, b in zip(v, f)])
            coupling = cpl[sub, z]
            for c in range(3):
                wgt[sub, c, z] = coupling * p[c]
                fix[sub, c, z, 0:32, 0:128] = p[c][0:32, 0:128]
                nxt[sub, c, z] = f[c][0:32, 0:128]
    for sub in range(2):
        for z in range(4):
            cobalt = spc[sub, z] == 1
            ratio = pick(cobalt, ratio_pair)
            p = [fix[sub, c, z, 0:32, 0:128] for c in range(3)]
            h = [
                ratio * neighbours(sub, c, z)[0:32, 0:128] + dpl[c, 0:32, 0:128] for c in range(3)
            ]
            h[2] = h[2] + pick(cobalt, EASY_PAIR) * p[2]
            f = torque(p, h)
            w = [
                vec[sub, c, z, 0:32, 0:128] + np.float32(0.5 * TIME_STEP) * (nxt[sub, c, z] + f[c])
                for c in range(3)
            ]
            w = normalized(w)
            for c in range(3):
                nxt[sub, c, z] = w[c]

    for halo in halo_all:
        halo.wait_send()
    blocks(b_a, nx - 1, s_a, r_a).wait_send()
    blocks(b_c, nx - 1, s_c, r_c).wait_send()
    blocks(b_b.at[core], chips - 1, s_b, r_b).wait_send()
    hand_on.wait_send()


def solution(mesh):
    nx, ny = mesh.shape["gx"], mesh.shape["gy"]
    table, corner = wave_tables(nx, ny)
    base, phase, twist, lanes = trig_tables(nx)
    vmem = pl.BlockSpec(memory_space=pltpu.VMEM)
    anywhere = pl.BlockSpec(memory_space=pl.ANY)
    dma = pltpu.SemaphoreType.DMA
    regular = pltpu.SemaphoreType.REGULAR

    def scratch(*shape, dtype=F32):
        return pltpu.VMEM(shape, dtype)

    def on_device(spin_angles, species):
        return pl.pallas_call(
            functools.partial(step_kernel, nx, ny, corner),
            out_shape=[
                jax.ShapeDtypeStruct((2, 3, 4, 32, 128), F32),
                jax.ShapeDtypeStruct((3, 1, 8, 32), F32),
            ],
            in_specs=[anywhere] * 3 + [vmem] * 4,
            out_specs=[vmem] * 2,
            scratch_shapes=[
                scratch(2, 2, 4, 32, 128),
                scratch(2, 4, 32, 128, dtype=jnp.int32),
                scratch(3, 32, 128),
                scratch(8, 128),
                scratch(nx, 8, 128),
                scratch(256, 128, dtype=BF16),
                scratch(256, 128, dtype=BF16),
                scratch(2, TABLE_ROWS, 128),
                scratch(2, TABLE_ROWS, 128),
                scratch(2, 8, 128),
                scratch(2, 8, 128),
                scratch(2, ny // 2, 2, 8, 128),
                scratch(nx, 16, 128),
                scratch(nx, 16, 128),
                scratch(2, 8, 128),
                scratch(2, 2, 4, 2, 128),
                scratch(2, 4, 2, 128, dtype=jnp.int32),
                scratch(2, 8, 128),
                scratch(2, 2, 8, 128),
                scratch(6, 4, 40, 256),
                scratch(2, 4, 40, 256),
                scratch(2, 3, 4, 40, 256),
                scratch(2, 3, 4, 40, 256),
                scratch(2, 3, 4, 40, 256),
                scratch(3, 40, 256),
                dma((6,)),
                dma, dma, dma, dma, dma, dma, dma, dma,
                dma((4,)),
                dma((4,)),
                regular((ny // 8,)),
                regular((ny // 8,)),
            ],
            compiler_params=pltpu.CompilerParams(collective_id=0, has_side_effects=True),
        )(spin_angles, species, table, base, phase, twist, lanes)

    return jax.shard_map(
        lambda a, s: tuple(on_device(a, s)),
        mesh=mesh,
        in_specs=(P(None, None, None, "gy", "gx"), P(None, None, "gy", "gx")),
        out_specs=(P(None, None, None, "gy", "gx"), P(None, None, "gy", "gx")),
        check_vma=False,
    )
```

```python
import functools
import math

import jax
import jax.numpy as jnp
import numpy as np
from jax import lax
from jax.experimental import pallas as pl
from jax.experimental.pallas import tpu as pltpu
from jax.sharding import PartitionSpec as P

MESH = pl.DeviceIdType.MESH
F32, BF16 = jnp.float32, jnp.bfloat16

CELLS_M = 4
DAMPING = 0.1
TIME_STEP = 0.05
EXCHANGE_SCALE = 0.6
DIPOLE = 2.0
MOMENT_PAIR = (2.22, 1.72)
COUPLING_PAIR = (1.0, 1.25)
ANISOTROPY_PAIR = (0.3, 0.9)
RATIO_PAIR = (COUPLING_PAIR[0] / MOMENT_PAIR[0], COUPLING_PAIR[1] / MOMENT_PAIR[1])
EASY_PAIR = (2 * ANISOTROPY_PAIR[0] / MOMENT_PAIR[0], 2 * ANISOTROPY_PAIR[1] / MOMENT_PAIR[1])

PART_K = 32
ROWS = 8
COLS = 32
GROUPS = 4
WINDOWS = 10
TABLE_LEAD = 8
TABLE_ROWS = 400


def wave_tables(nx, ny):
    period_x, period_y = 2 * nx * COLS, 2 * ny * ROWS
    half_y = period_y // 2
    v = np.arange(period_x // 2 + 1)
    u = np.arange(half_y + 1)
    a = 2 * np.pi * v[:, None] / period_x
    b = 2 * np.pi * u[None, :] / period_y
    k = np.sqrt(a * a + b * b)
    inv = np.where(k > 0, 1.0 / np.where(k > 0, k, 1.0), 0.0)
    g = {
        "xx": -a * a * 0.5 * inv,
        "yy": -b * b * 0.5 * inv,
        "zz": 0.5 * k - 1.0,
        "xy": -a * b * 0.5 * inv,
    }
    dy = np.arange(-TABLE_LEAD, TABLE_ROWS - TABLE_LEAD)
    angle = 2 * np.pi * ((u[:, None] * dy[None, :]) % period_y) / period_y
    fold = np.where((u == 0) | (u == half_y), 1.0, 2.0)
    cosine = fold[:, None] * np.cos(angle)
    sine = np.where((u == 0) | (u == half_y), 0.0, 2.0)[:, None] * np.sin(angle)
    scale = DIPOLE / (period_x * period_y) * np.where((v == 0) | (v == period_x // 2), 1.0, 2.0)
    tables = [scale[:, None] * (g[n] @ cosine) for n in ("xx", "yy", "zz")]
    odd = scale[:, None] * (g["xy"] @ sine)
    odd[-1] = 0.0
    tables.append(odd)
    lanes = np.stack(tables)
    out = np.zeros((nx + 1, TABLE_ROWS, 4 * PART_K), np.float32)
    for s in range(nx):
        block = lanes[:, s * PART_K : (s + 1) * PART_K, :]
        out[s] = block.transpose(2, 0, 1).reshape(TABLE_ROWS, -1)
    out[nx] = out[0]
    for n in range(4):
        out[nx, :, n * PART_K] = lanes[n, -1, :]
    corner = DIPOLE / (period_x * period_y) * float(-0.5 * np.pi * np.pi / np.sqrt(2 * np.pi**2))
    return out, corner


def trig_tables(nx):
    period = 2 * nx * COLS
    lane = np.arange(128)
    comp = np.where(lane < 96, lane // 32, np.where(lane < 102, (lane - 96) // 2, 3))
    place = np.where(lane < 96, lane % 32, np.where(lane % 2 == 0, -1, 32))
    j = np.arange(PART_K)
    t = 2 * np.pi * ((j[:, None] * place[None, :]) % period) / period
    base = np.stack([np.cos(t), np.sin(t)]).astype(np.float32)
    s = np.arange(nx)
    t = 2 * np.pi * ((s[:, None] * PART_K * place[None, :]) % period) / period
    phase = np.stack([np.cos(t), np.sin(t)], axis=1).astype(np.float32)
    jl = lane % 32
    t = 2 * np.pi * ((s[:, None] * COLS * jl[None, :]) % period) / period
    twist = np.stack([np.cos(t), np.sin(t)]).astype(np.float32)
    row = np.stack([comp, np.where(place % 2 == 0, 1, -1)]).astype(np.float32)
    return base, phase, twist, row


def sine(r):
    q = r * r
    p = 1.0 / 6227020800.0
    for c in (-1.0 / 39916800.0, 1.0 / 362880.0, -1.0 / 5040.0, 1.0 / 120.0, -1.0 / 6.0):
        p = p * q + c
    return r + r * q * p


def sine_cosine(x):
    size = jnp.abs(x)
    far = (np.float32(math.pi) - size) + np.float32(math.pi - float(np.float32(math.pi)))
    s = sine(jnp.where(size > np.float32(math.pi / 2), far, size))
    half = (np.float32(math.pi / 2) - size) + np.float32(
        math.pi / 2 - float(np.float32(math.pi / 2))
    )
    return jnp.where(x < 0, -s, s), sine(half)


def pick(cobalt, pair):
    return jnp.where(cobalt, np.float32(pair[1]), np.float32(pair[0]))


def unit(polar, azimuth):
    sp, cp = sine_cosine(polar)
    sq, cq = sine_cosine(azimuth)
    return sp * cq, sp * sq, cp


def iota(shape, dim):
    return lax.broadcasted_iota(jnp.int32, shape, dim)


def cross(a, b):
    return (
        a[1] * b[2] - a[2] * b[1],
        a[2] * b[0] - a[0] * b[2],
        a[0] * b[1] - a[1] * b[0],
    )


def torque(v, h):
    p = cross(v, h)
    r = cross(v, p)
    return [
        (a + np.float32(DAMPING) * b) * np.float32(-1.0 / (1.0 + DAMPING * DAMPING))
        for a, b in zip(p, r)
    ]


def normalized(w):
    s = w[0] * w[0] + w[1] * w[1] + w[2] * w[2]
    r = lax.rsqrt(s)
    r = r * (1.5 - 0.5 * s * r * r)
    return [c * r for c in w]


def split(x, pieces):
    out = []
    for _ in range(pieces):
        out.append(x.astype(BF16))
        x = x - out[-1].astype(F32)
    return out


def dot(a, b, dims=(1, 0)):
    return lax.dot_general(
        a, b, (((dims[0],), (dims[1],)), ((), ())), preferred_element_type=F32
    )


def exact_dot(a, hot):
    n = a.shape[0]
    out = dot(jnp.concatenate(split(a, 3), axis=0), hot)
    return out[0:n] + out[n : 2 * n] + out[2 * n : 3 * n]


def wide_dot(a, b_high, b_low, dims):
    n = a.shape[0]
    high, low = split(a, 2)
    out = dot(jnp.concatenate([high, low], axis=0), b_high, dims)
    return out[0:n] + out[n : 2 * n] + dot(high, b_low, dims)


def step_kernel(
    nx, ny, corner,
    ang_hbm, spc_hbm, table_hbm, base, phase, twist, lanes,
    nxt, dip,
    ang, spc, mom, tile, b_a, q_high, q_low, tab, tab2, up, dn, b_b, send_c, b_c, pack, g_ang, g_spc, g_x, g_c,
    raw, cpl, vec, wgt, fix, dpl,
    load_sem, s_a, r_a, s_b, r_b, s_f, r_f, s_c, r_c, s_h, r_h, word,
):
    gx, gy = lax.axis_index("gx"), lax.axis_index("gy")
    left, right = lax.rem(gx + nx - 1, nx), lax.rem(gx + 1, nx)
    below, above = lax.rem(gy + ny - 1, ny), lax.rem(gy + 1, ny)
    core = lax.rem(gy, 2)
    chip = gy // 2
    partner = gy + 1 - 2 * core
    chips = ny // 2
    nz = ny // 4
    hops = nz // 2
    side, z_own = chip // nz, lax.rem(chip, nz)

    def at(across, dz):
        there = (1 - side) if across else side
        return 2 * (nz * there + lax.rem(z_own + dz + nz, nz)) + core

    group = chips // GROUPS

    loads = []
    for sub in range(2):
        loads.append(pltpu.make_async_copy(ang_hbm.at[sub], ang.at[sub], load_sem.at[2 * sub]))
        loads.append(pltpu.make_async_copy(spc_hbm.at[sub], spc.at[sub], load_sem.at[2 * sub + 1]))
    late_loads = [
        pltpu.make_async_copy(table_hbm.at[gx], tab.at[0], load_sem.at[4]),
        pltpu.make_async_copy(table_hbm.at[jnp.where(gx == 0, nx, gx)], tab.at[1], load_sem.at[5]),
    ]
    for load in loads + late_loads:
        load.start()

    barrier = pltpu.get_barrier_semaphore()

    def signal(semaphore, device):
        pl.semaphore_signal(semaphore, inc=1, device_id=device, device_id_type=MESH)

    @pl.loop(1, nx)
    def _(o):
        signal(barrier, (lax.rem(gx + o, nx), gy))

    near = [above, below, at(True, 0), at(True, 1), at(True, -1)]
    for dz in range(1, hops):
        near += [at(False, dz), at(False, -dz)]
    for other in near:
        signal(barrier, (gx, other))

    def remote(src, dst, send, recv, device):
        return pltpu.make_async_remote_copy(
            src_ref=src, dst_ref=dst, send_sem=send, recv_sem=recv, device_id=device, device_id_type=MESH
        )

    b_cos, b_sin = base[0], base[1]
    p_cos, p_sin = phase[gx, 0:1, :], phase[gx, 1:2, :]
    cosine = b_cos * p_cos - b_sin * p_sin
    sinus = b_sin * p_cos + b_cos * p_sin
    comp, parity = lanes[0:1, :], lanes[1:2, :]
    single = (iota((32, 128), 0) + gx) == 0

    def store_q(at, q):
        q_high[pl.ds(at, 32), :], q_low[pl.ds(at, 32), :] = split(q, 2)

    for c in range(3):
        mine = comp == np.float32(c)
        real, imag = (sinus, cosine) if c == 1 else (cosine, -sinus)
        store_q(32 * c, jnp.where(mine, jnp.where(single, 1.0, real), 0.0))
        store_q(128 + 32 * c, jnp.where(mine, jnp.where(single, parity, imag), 0.0))
    store_q(96, jnp.zeros((32, 128), F32))
    store_q(224, jnp.zeros((32, 128), F32))

    total = [jnp.zeros((32, 128), F32) for _ in range(3)]
    for sub in range(2):
        loads[2 * sub].wait()
        loads[2 * sub + 1].wait()
        for z in range(4):
            moment = pick(spc[sub, z] == 1, MOMENT_PAIR)
            v = unit(ang[sub, 0, z], ang[sub, 1, z])
            for c in range(3):
                vec[sub, c, z, 0:32, 0:128] = v[c]
            total = [t + moment * c for t, c in zip(total, v)]
    rows = []
    for c in range(3):
        mom[c] = total[c]
        line = mom[c, pl.ds(0, 8, 4), :]
        for r in range(1, 4):
            line = line + mom[c, pl.ds(r, 8, 4), :]
        rows.append(line)
    atom = iota((384, 128), 0)
    place = ((atom >> 7) << 5) + ((atom & 127) >> 2)
    spread = jnp.where(iota((384, 128), 1) == place, 1 / 128, 0.0).astype(BF16)
    packed = exact_dot(jnp.concatenate(rows, axis=1), spread)
    tile[...] = packed

    pl.semaphore_wait(barrier, nx - 1 + len(near))

    @pl.loop(1, nx)
    def _(o):
        remote(tile, b_a.at[gx], s_a, r_a, (lax.rem(gx + o, nx), gy)).start()

    signal(word.at[0], (gx, at(True, 0)))
    signal(word.at[1], (gx, at(False, -1)))
    signal(word.at[2], (gx, at(True, -1)))

    halo_row, halo_spc, halo_x, halo_c = [
        [remote(src, dst, s_h.at[n], r_h.at[n], to) for src, dst, to in pair]
        for n, pair in enumerate((
            ((ang.at[:, :, :, pl.ds(31, 1), :], g_ang.at[:, :, :, pl.ds(0, 1), :], (gx, above)),
             (ang.at[:, :, :, pl.ds(0, 1), :], g_ang.at[:, :, :, pl.ds(1, 1), :], (gx, below))),
            ((spc.at[:, :, pl.ds(31, 1), :], g_spc.at[:, :, pl.ds(0, 1), :], (gx, above)),
             (spc.at[:, :, pl.ds(0, 1), :], g_spc.at[:, :, pl.ds(1, 1), :], (gx, below))),
            ((pack.at[1], g_x.at[0], (right, gy)), (pack.at[0], g_x.at[1], (left, gy))),
            ((g_x, g_c.at[0], (gx, above)), (g_x, g_c.at[1], (gx, below))),
        ))
    ]
    halo_all = [remote(g, g, s_h.at[n], r_h.at[n], (gx, gy)) for n, g in enumerate((g_ang, g_spc, g_x, g_c))]

    b_a[gx] = packed

    lane = iota((128, 128), 1)
    edges = jnp.zeros((128, 128), F32)
    for q in range(3):
        for sub in range(2):
            n = 2 * q + sub
            block = ang[sub, q] if q < 2 else spc[sub].astype(F32)
            block = block.reshape(128, 128)
            edges = jnp.where(lane == n, pltpu.roll(block, n, 1) if n else block, edges)
            edges = jnp.where(lane == 8 + n, pltpu.roll(block, n + 9, 1), edges)
    edges = jnp.transpose(edges)
    pack[0] = edges[0:8]
    pack[1] = edges[8:16]
    for copy in halo_x + halo_row + halo_spc:
        copy.start()

    def blocks(ref, n, send, recv):
        return remote(ref.at[pl.ds(0, n)], ref.at[pl.ds(0, n)], send, recv, (gx, gy))

    blocks(b_a, nx - 1, s_a, r_a).wait_recv()

    wave = wide_dot(b_a[...].reshape(nx * 8, 128), q_high[...], q_low[...], (1, 1))
    real = jnp.zeros((8, 128), F32)
    imag = jnp.zeros((8, 128), F32)
    for g in range(nx):
        t_re, t_im = wave[8 * g : 8 * g + 8, 0:128], wave[8 * g : 8 * g + 8, 128:256]
        c, s = twist[0, g : g + 1, :], twist[1, g : g + 1, :]
        real = real + (t_re * c + t_im * s)
        imag = imag + (t_im * c - t_re * s)

    lane8 = iota((8, 128), 1)
    is_y = (lane8 >= 32) & (lane8 < 64)
    flip = jnp.where(is_y, np.float32(-1), np.float32(1))
    dn[0] = real * flip
    dn[1] = imag * flip
    for r in range(8):
        up[0, r : r + 1, :] = real[7 - r : 8 - r]
        up[1, r : r + 1, :] = imag[7 - r : 8 - r]

    for n in range(3):
        pl.semaphore_wait(word.at[n], 1)

    @pl.loop(0, chips - 1)
    def _(k):
        slot = chips - 1 - k
        n, a = slot // 2, lax.rem(slot, 2)
        odd = lax.rem(n, 2) == 1
        steps = jnp.where(odd, (n + 1) // 2, nz - n // 2)
        back = jnp.where((n == 0) | (n == nz - 1), n, jnp.where(odd, n + 1, n - 1))
        there = 2 * back + a
        to_chip = nz * jnp.where(a == 1, 1 - side, side) + lax.rem(z_own + steps, nz)
        to = 2 * to_chip + core
        land, mark = b_b.at[core, there], r_b.at[there // group]

        @pl.when(to > gy)
        def _():
            remote(up, land, s_b, mark, (gx, to)).start()

        @pl.when(to < gy)
        def _():
            remote(dn, land, s_b, mark, (gx, to)).start()

    even = core == 0
    b_b[core, 0] = jnp.where(even, up[...], dn[...])

    for load in late_loads:
        load.wait()
    wide = iota((TABLE_ROWS, 128), 1)
    for p in range(2):
        t = tab[p]
        tab2[p] = jnp.where(
            wide < 32,
            pltpu.roll(t, 32, 1),
            jnp.where(wide < 64, -pltpu.roll(t, 64, 1), 0.0),
        )

    halo_all[2].wait_recv()
    for copy in halo_c:
        copy.start()
    halo_all[0].wait_recv()
    halo_all[1].wait_recv()
    halo_all[3].wait_recv()

    cols = jnp.concatenate(
        [g_x[0], g_x[1], g_c[0, 0], g_c[0, 1], g_c[1, 0], g_c[1, 1], jnp.zeros((80, 128), F32)], axis=0
    )
    cols = jnp.transpose(cols)
    lane32 = iota((32, 128), 1)
    rowh = iota((8, 128), 0)
    for q in range(3):
        for sub in range(2):
            n = 2 * q + sub
            for z in range(4):

                def column(piece):
                    part = cols[32 * z : 32 * z + 32, 8 * piece + n : 8 * piece + n + 1]
                    return jnp.broadcast_to(part, (32, 128))

                def spot(piece, y):
                    part = cols[32 * z + y : 32 * z + y + 1, 8 * piece + n : 8 * piece + n + 1]
                    return jnp.broadcast_to(part, (8, 128))

                def edge(side):
                    if q < 2:
                        return jnp.broadcast_to(g_ang[sub, q, z, side : side + 1, :], (8, 128))
                    return jnp.broadcast_to(g_spc[sub, z, side : side + 1, :], (8, 128)).astype(F32)

                if q == 2:
                    raw[n, z, 0:32, 0:128] = spc[sub, z].astype(F32)
                raw[n, z, 0:32, 128:256] = jnp.where(lane32 < 64, column(1), column(0))
                raw[n, z, 32:40, 0:128] = jnp.where(rowh < 4, edge(1), edge(0))
                low = jnp.where(lane8 < 64, spot(3, 31), spot(2, 31))
                high = jnp.where(lane8 < 64, spot(5, 0), spot(4, 0))
                raw[n, z, 32:40, 128:256] = jnp.where(rowh < 4, high, low)

    at_row = iota((40, 256), 0)
    at_col = iota((40, 256), 1)
    y = gy * 32 + jnp.where(at_row < 36, at_row, at_row - 40)
    x = gx * 128 + jnp.where(at_col < 192, at_col, at_col - 256)
    inside = (y >= 0) & (y < ny * 32) & (x >= 0) & (x < nx * 128)
    for sub in range(2):
        for z in range(4):
            for r, l in ((slice(0, 32), slice(128, 256)), (slice(32, 40), slice(0, 256))):
                v = unit(raw[sub, z, r, l], raw[2 + sub, z, r, l])
                for c in range(3):
                    vec[sub, c, z, r, l] = v[c]
            coupling = jnp.where(inside, pick(raw[4 + sub, z] > 0.5, COUPLING_PAIR), 0.0)
            cpl[sub, z] = coupling
            for c in range(3):
                wgt[sub, c, z] = coupling * vec[sub, c, z]

    def neighbours(sub, c, z):
        other = 1 - sub
        near = wgt[other, c, z]
        far = z - 1 if sub == 0 else z + 1
        if 0 <= far < 4:
            near = near + wgt[other, c, far]
        near = near + pltpu.roll(near, 1 if sub == 0 else 255, 1)
        return near + pltpu.roll(near, 1 if sub == 0 else 39, 0)

    ratio_pair = [np.float32(EXCHANGE_SCALE) * np.float32(r) for r in RATIO_PAIR]
    for sub in range(2):
        for z in range(4):
            cobalt = raw[4 + sub, z] > 0.5
            ratio = pick(cobalt, ratio_pair)
            for c in range(3):
                h = ratio * neighbours(sub, c, z)
                if c == 2:
                    h = h + pick(cobalt, EASY_PAIR) * vec[sub, c, z]
                fix[sub, c, z] = h

    def hand_on(g):
        part = b_b.at[core, pl.ds(group * g, group)]
        return remote(part, part, s_f.at[g], r_f.at[g], (gx, partner))

    for g in range(GROUPS):
        blocks(b_b.at[core], group - (g == 0), s_b, r_b.at[g]).wait_recv()
        hand_on(g).start()

    zero = jnp.zeros((8, 128), F32)

    def swapped(s):
        return jnp.where(lane8 < 32, pltpu.roll(s, 96, 1), pltpu.roll(s, 32, 1))

    def add_source(d, parts, acc):
        acc = list(acc)
        for p in range(2):
            s = parts[p]
            t = swapped(s)
            for w in range(WINDOWS):
                span = pl.ds(8 * d + w, 8)
                acc[2 * w + p] = acc[2 * w + p] + tab[p, span, :] * s + tab2[p, span, :] * t
        acc[-1] = acc[-1] + parts[1]
        return tuple(acc)

    def add_chips(which, acc_up, acc_dn):
        def source(k):
            ahead = lax.rem(lax.rem(k, nz) - z_own + nz, nz)
            n = jnp.where(
                ahead == 0, 0, jnp.where(ahead <= hops, 2 * ahead - 1, 2 * (nz - ahead))
            )
            slot = 2 * n + jnp.where(k // nz == side, 0, 1)
            return b_b[which, slot, 0], b_b[which, slot, 1]

        acc_up = lax.fori_loop(
            0, chip, lambda k, a: add_source(gy - (2 * k + which), source(k), a), acc_up
        )
        acc_dn = lax.fori_loop(
            chip + 1, chips, lambda k, a: add_source(2 * k + which - gy, source(k), a), acc_dn
        )
        return acc_up, acc_dn

    start = tuple(zero for _ in range(2 * WINDOWS + 1))
    acc_up = add_source(0, (up[0], up[1]), start)
    acc_up, acc_dn = add_chips(core, acc_up, start)
    for g in range(GROUPS):
        hand_on(g).wait_recv()
    acc_up, acc_dn = add_chips(1 - core, acc_up, acc_dn)
    beside = (b_b[1 - core, 0, 0], b_b[1 - core, 0, 1])
    acc_up = lax.fori_loop(0, core, lambda _, a: add_source(1, beside, a), acc_up)
    acc_dn = lax.fori_loop(0, 1 - core, lambda _, a: add_source(1, beside, a), acc_dn)

    alternate = jnp.where(iota((8, 128), 0) % 2 == 0, np.float32(1), np.float32(-1))
    last = jnp.sum((flip * acc_dn[-1] - acc_up[-1]) * alternate, axis=0, keepdims=True)
    last = jnp.broadcast_to(last, (8, 128))
    last = swapped(last)
    last = jnp.where(((lane8 == 0) | (lane8 == 32)) & (gx == 0), last, 0.0) * np.float32(corner)

    row16 = iota((16, 128), 0)
    field = []
    for p in range(2):
        out = jnp.zeros((16, 128), F32)
        for w in range(WINDOWS):
            sums = acc_up[2 * w + p] + flip * acc_dn[2 * (WINDOWS - 1 - w) + p]
            if p == 1:
                sign = np.float32((1 if w % 2 else -1) / 8)
                sums = sums + sign * last
            line = jnp.sum(sums, axis=0, keepdims=True)
            out = jnp.where(row16 == w, jnp.broadcast_to(line, (16, 128)), out)
        field.append(out)

    turned = []
    for g in range(nx):
        c, s = twist[0, g : g + 1, :], twist[1, g : g + 1, :]
        turned.append(
            jnp.concatenate([field[0] * c - field[1] * s, field[0] * s + field[1] * c], axis=1)
        )
    shares = wide_dot(jnp.concatenate(turned, axis=0), q_high[...], q_low[...], (1, 0))
    send_c[...] = shares.reshape(nx, 16, 128)

    @pl.loop(1, nx)
    def _(o):
        to = lax.rem(gx + o, nx)
        part = pl.ds(0, WINDOWS)
        remote(send_c.at[to, part], b_c.at[gx, part], s_c, r_c, (to, gy)).start()

    b_c[gx] = send_c[gx]
    atom = iota((128, 256), 1)
    want = jnp.where(atom < 128, atom >> 2, jnp.where(atom < 192, 97, 96))
    scale = jnp.where(atom < 128, 32, 2)
    hot = [
        jnp.where(iota((128, 256), 0) == want + scale * c, 1.0, 0.0).astype(BF16) for c in range(3)
    ]
    row8 = iota((8, 256), 0)

    all_c = b_c.at[pl.ds(0, nx - 1), pl.ds(0, WINDOWS)]
    shares_in = remote(all_c, all_c, s_c, r_c, (gx, gy))
    shares_in.wait_recv()
    whole = b_c[0]
    for g in range(1, nx):
        whole = whole + b_c[g]

    for c in range(3):
        dip[c, 0] = whole[1:9, 32 * c : 32 * c + 32]
        lines = exact_dot(whole, hot[c])

        def line(w):
            return jnp.broadcast_to(lines[w : w + 1], (8, 256))

        for t in range(4):
            dpl[c, pl.ds(8 * t, 8), :] = jnp.where(row8 < 4, line(2 * t + 1), line(2 * t + 2))
        dpl[c, pl.ds(32, 8), :] = jnp.where(row8 < 4, line(9), line(0))

    for sub in range(2):
        for z in range(4):
            v = [vec[sub, c, z] for c in range(3)]
            f = torque(v, [fix[sub, c, z] + dpl[c] for c in range(3)])
            p = normalized([a + np.float32(TIME_STEP) * b for a, b in zip(v, f)])
            coupling = cpl[sub, z]
            for c in range(3):
                wgt[sub, c, z] = coupling * p[c]
                fix[sub, c, z, 0:32, 0:128] = p[c][0:32, 0:128]
                nxt[sub, c, z] = f[c][0:32, 0:128]
    for sub in range(2):
        for z in range(4):
            cobalt = spc[sub, z] == 1
            ratio = pick(cobalt, ratio_pair)
            p = [fix[sub, c, z, 0:32, 0:128] for c in range(3)]
            h = [
                ratio * neighbours(sub, c, z)[0:32, 0:128] + dpl[c, 0:32, 0:128] for c in range(3)
            ]
            h[2] = h[2] + pick(cobalt, EASY_PAIR) * p[2]
            f = torque(p, h)
            w = [
                vec[sub, c, z, 0:32, 0:128] + np.float32(0.5 * TIME_STEP) * (nxt[sub, c, z] + f[c])
                for c in range(3)
            ]
            w = normalized(w)
            for c in range(3):
                nxt[sub, c, z] = w[c]

    for halo in halo_all:
        halo.wait_send()
    blocks(b_a, nx - 1, s_a, r_a).wait_send()
    shares_in.wait_send()
    blocks(b_b.at[core], chips - 1, s_b, r_b.at[0]).wait_send()
    for g in range(GROUPS):
        hand_on(g).wait_send()


def solution(mesh):
    nx, ny = mesh.shape["gx"], mesh.shape["gy"]
    table, corner = wave_tables(nx, ny)
    base, phase, twist, lanes = trig_tables(nx)
    vmem = pl.BlockSpec(memory_space=pltpu.VMEM)
    anywhere = pl.BlockSpec(memory_space=pl.ANY)
    dma = pltpu.SemaphoreType.DMA
    regular = pltpu.SemaphoreType.REGULAR

    def scratch(*shape, dtype=F32):
        return pltpu.VMEM(shape, dtype)

    def on_device(spin_angles, species):
        return pl.pallas_call(
            functools.partial(step_kernel, nx, ny, corner),
            out_shape=[
                jax.ShapeDtypeStruct((2, 3, 4, 32, 128), F32),
                jax.ShapeDtypeStruct((3, 1, 8, 32), F32),
            ],
            in_specs=[anywhere] * 3 + [vmem] * 4,
            out_specs=[vmem] * 2,
            scratch_shapes=[
                scratch(2, 2, 4, 32, 128),
                scratch(2, 4, 32, 128, dtype=jnp.int32),
                scratch(3, 32, 128),
                scratch(8, 128),
                scratch(nx, 8, 128),
                scratch(256, 128, dtype=BF16),
                scratch(256, 128, dtype=BF16),
                scratch(2, TABLE_ROWS, 128),
                scratch(2, TABLE_ROWS, 128),
                scratch(2, 8, 128),
                scratch(2, 8, 128),
                scratch(2, ny // 2, 2, 8, 128),
                scratch(nx, 16, 128),
                scratch(nx, 16, 128),
                scratch(2, 8, 128),
                scratch(2, 2, 4, 2, 128),
                scratch(2, 4, 2, 128, dtype=jnp.int32),
                scratch(2, 8, 128),
                scratch(2, 2, 8, 128),
                scratch(6, 4, 40, 256),
                scratch(2, 4, 40, 256),
                scratch(2, 3, 4, 40, 256),
                scratch(2, 3, 4, 40, 256),
                scratch(2, 3, 4, 40, 256),
                scratch(3, 40, 256),
                dma((6,)),
                dma, dma, dma, dma((GROUPS,)), dma((GROUPS,)), dma((GROUPS,)), dma, dma,
                dma((4,)),
                dma((4,)),
                regular((3,)),
            ],
            compiler_params=pltpu.CompilerParams(collective_id=0, has_side_effects=True),
        )(spin_angles, species, table, base, phase, twist, lanes)

    return jax.shard_map(
        lambda a, s: tuple(on_device(a, s)),
        mesh=mesh,
        in_specs=(P(None, None, None, "gy", "gx"), P(None, None, "gy", "gx")),
        out_specs=(P(None, None, None, "gy", "gx"), P(None, None, "gy", "gx")),
        check_vma=False,
    )
```

```python
import functools
import math

import jax
import jax.numpy as jnp
import numpy as np
from jax import lax
from jax.experimental import pallas as pl
from jax.experimental.pallas import tpu as pltpu
from jax.sharding import PartitionSpec as P

MESH = pl.DeviceIdType.MESH
F32, BF16 = jnp.float32, jnp.bfloat16

CELLS_M = 4
DAMPING = 0.1
TIME_STEP = 0.05
EXCHANGE_SCALE = 0.6
DIPOLE = 2.0
MOMENT_PAIR = (2.22, 1.72)
COUPLING_PAIR = (1.0, 1.25)
ANISOTROPY_PAIR = (0.3, 0.9)
RATIO_PAIR = (COUPLING_PAIR[0] / MOMENT_PAIR[0], COUPLING_PAIR[1] / MOMENT_PAIR[1])
EASY_PAIR = (2 * ANISOTROPY_PAIR[0] / MOMENT_PAIR[0], 2 * ANISOTROPY_PAIR[1] / MOMENT_PAIR[1])

PART_K = 32
ROWS = 8
COLS = 32
GROUPS = 4
WINDOWS = 10
TABLE_LEAD = 8
TABLE_ROWS = 400


def wave_tables(nx, ny):
    period_x, period_y = 2 * nx * COLS, 2 * ny * ROWS
    half_y = period_y // 2
    v = np.arange(period_x // 2 + 1)
    u = np.arange(half_y + 1)
    a = 2 * np.pi * v[:, None] / period_x
    b = 2 * np.pi * u[None, :] / period_y
    k = np.sqrt(a * a + b * b)
    inv = np.where(k > 0, 1.0 / np.where(k > 0, k, 1.0), 0.0)
    g = {
        "xx": -a * a * 0.5 * inv,
        "yy": -b * b * 0.5 * inv,
        "zz": 0.5 * k - 1.0,
        "xy": -a * b * 0.5 * inv,
    }
    dy = np.arange(-TABLE_LEAD, TABLE_ROWS - TABLE_LEAD)
    angle = 2 * np.pi * ((u[:, None] * dy[None, :]) % period_y) / period_y
    fold = np.where((u == 0) | (u == half_y), 1.0, 2.0)
    cosine = fold[:, None] * np.cos(angle)
    sine = np.where((u == 0) | (u == half_y), 0.0, 2.0)[:, None] * np.sin(angle)
    scale = DIPOLE / (period_x * period_y) * np.where((v == 0) | (v == period_x // 2), 1.0, 2.0)
    tables = [scale[:, None] * (g[n] @ cosine) for n in ("xx", "yy", "zz")]
    odd = scale[:, None] * (g["xy"] @ sine)
    odd[-1] = 0.0
    tables.append(odd)
    lanes = np.stack(tables)
    out = np.zeros((nx + 1, TABLE_ROWS, 4 * PART_K), np.float32)
    for s in range(nx):
        block = lanes[:, s * PART_K : (s + 1) * PART_K, :]
        out[s] = block.transpose(2, 0, 1).reshape(TABLE_ROWS, -1)
    out[nx] = out[0]
    for n in range(4):
        out[nx, :, n * PART_K] = lanes[n, -1, :]
    corner = DIPOLE / (period_x * period_y) * float(-0.5 * np.pi * np.pi / np.sqrt(2 * np.pi**2))
    return out, corner


def trig_tables(nx):
    period = 2 * nx * COLS
    lane = np.arange(128)
    comp = np.where(lane < 96, lane // 32, np.where(lane < 102, (lane - 96) // 2, 3))
    place = np.where(lane < 96, lane % 32, np.where(lane % 2 == 0, -1, 32))
    j = np.arange(PART_K)
    t = 2 * np.pi * ((j[:, None] * place[None, :]) % period) / period
    base = np.stack([np.cos(t), np.sin(t)]).astype(np.float32)
    s = np.arange(nx)
    t = 2 * np.pi * ((s[:, None] * PART_K * place[None, :]) % period) / period
    phase = np.stack([np.cos(t), np.sin(t)], axis=1).astype(np.float32)
    jl = lane % 32
    t = 2 * np.pi * ((s[:, None] * COLS * jl[None, :]) % period) / period
    twist = np.stack([np.cos(t), np.sin(t)]).astype(np.float32)
    row = np.stack([comp, np.where(place % 2 == 0, 1, -1)]).astype(np.float32)
    return base, phase, twist, row


def sine(r):
    q = r * r
    p = 1.0 / 6227020800.0
    for c in (-1.0 / 39916800.0, 1.0 / 362880.0, -1.0 / 5040.0, 1.0 / 120.0, -1.0 / 6.0):
        p = p * q + c
    return r + r * q * p


def sine_cosine(x):
    size = jnp.abs(x)
    far = (np.float32(math.pi) - size) + np.float32(math.pi - float(np.float32(math.pi)))
    s = sine(jnp.where(size > np.float32(math.pi / 2), far, size))
    half = (np.float32(math.pi / 2) - size) + np.float32(
        math.pi / 2 - float(np.float32(math.pi / 2))
    )
    return jnp.where(x < 0, -s, s), sine(half)


def pick(cobalt, pair):
    return jnp.where(cobalt, np.float32(pair[1]), np.float32(pair[0]))


def unit(polar, azimuth):
    sp, cp = sine_cosine(polar)
    sq, cq = sine_cosine(azimuth)
    return sp * cq, sp * sq, cp


def iota(shape, dim):
    return lax.broadcasted_iota(jnp.int32, shape, dim)


def cross(a, b):
    return (
        a[1] * b[2] - a[2] * b[1],
        a[2] * b[0] - a[0] * b[2],
        a[0] * b[1] - a[1] * b[0],
    )


def torque(v, h):
    p = cross(v, h)
    r = cross(v, p)
    return [
        (a + np.float32(DAMPING) * b) * np.float32(-1.0 / (1.0 + DAMPING * DAMPING))
        for a, b in zip(p, r)
    ]


def normalized(w):
    s = w[0] * w[0] + w[1] * w[1] + w[2] * w[2]
    r = lax.rsqrt(s)
    r = r * (1.5 - 0.5 * s * r * r)
    return [c * r for c in w]


def split(x, pieces):
    out = []
    for _ in range(pieces):
        out.append(x.astype(BF16))
        x = x - out[-1].astype(F32)
    return out


def dot(a, b, dims=(1, 0)):
    return lax.dot_general(
        a, b, (((dims[0],), (dims[1],)), ((), ())), preferred_element_type=F32
    )


def exact_dot(a, hot):
    n = a.shape[0]
    out = dot(jnp.concatenate(split(a, 3), axis=0), hot)
    return out[0:n] + out[n : 2 * n] + out[2 * n : 3 * n]


def wide_dot(a, b_high, b_low, dims):
    n = a.shape[0]
    high, low = split(a, 2)
    out = dot(jnp.concatenate([high, low], axis=0), b_high, dims)
    return out[0:n] + out[n : 2 * n] + dot(high, b_low, dims)


def step_kernel(
    nx, ny, corner,
    ang_hbm, spc_hbm, table_hbm, base_hbm, phase_hbm, twist_hbm, lanes_hbm,
    nxt, fld,
    base, phase, twist, lanes, ang, spc, mom, tile, b_a, q_high, q_low, tab, tab2, up, dn, b_b, send_c, b_c, pack, g_ang, g_spc, g_x, g_c,
    raw, cpl, vec, wgt, fix, dpl,
    load_sem, s_a, r_a, s_b, r_b, s_f, r_f, s_c, r_c, s_h, r_h, word,
):
    gx, gy = lax.axis_index("gx"), lax.axis_index("gy")
    left, right = lax.rem(gx + nx - 1, nx), lax.rem(gx + 1, nx)
    below, above = lax.rem(gy + ny - 1, ny), lax.rem(gy + 1, ny)
    core = lax.rem(gy, 2)
    chip = gy // 2
    partner = gy + 1 - 2 * core
    chips = ny // 2
    nz = ny // 4
    hops = nz // 2
    side, z_own = chip // nz, lax.rem(chip, nz)

    def at(across, dz):
        there = (1 - side) if across else side
        return 2 * (nz * there + lax.rem(z_own + dz + nz, nz)) + core

    group = chips // GROUPS

    loads = []
    for sub in range(2):
        loads.append(pltpu.make_async_copy(ang_hbm.at[sub], ang.at[sub], load_sem.at[2 * sub]))
        loads.append(pltpu.make_async_copy(spc_hbm.at[sub], spc.at[sub], load_sem.at[2 * sub + 1]))
    late_loads = [
        pltpu.make_async_copy(table_hbm.at[gx], tab.at[0], load_sem.at[4]),
        pltpu.make_async_copy(table_hbm.at[jnp.where(gx == 0, nx, gx)], tab.at[1], load_sem.at[5]),
    ]
    small_loads = [
        pltpu.make_async_copy(src, dst, load_sem.at[6 + n])
        for n, (src, dst) in enumerate(
            ((base_hbm, base), (phase_hbm.at[gx], phase), (lanes_hbm, lanes), (twist_hbm, twist))
        )
    ]
    for load in small_loads + loads + late_loads:
        load.start()

    barrier = pltpu.get_barrier_semaphore()

    def signal(semaphore, device):
        pl.semaphore_signal(semaphore, inc=1, device_id=device, device_id_type=MESH)

    @pl.loop(1, nx)
    def _(o):
        signal(barrier, (lax.rem(gx + o, nx), gy))

    near = [above, below, at(True, 0), at(True, 1), at(True, -1)]
    for dz in range(1, hops):
        near += [at(False, dz), at(False, -dz)]
    for other in near:
        signal(barrier, (gx, other))

    def remote(src, dst, send, recv, device):
        return pltpu.make_async_remote_copy(
            src_ref=src, dst_ref=dst, send_sem=send, recv_sem=recv, device_id=device, device_id_type=MESH
        )

    for load in small_loads:
        load.wait()
    b_cos, b_sin = base[0], base[1]
    p_cos, p_sin = phase[0:1, :], phase[1:2, :]
    cosine = b_cos * p_cos - b_sin * p_sin
    sinus = b_sin * p_cos + b_cos * p_sin
    comp, parity = lanes[0:1, :], lanes[1:2, :]
    single = (iota((32, 128), 0) + gx) == 0

    def store_q(at, q):
        q_high[pl.ds(at, 32), :], q_low[pl.ds(at, 32), :] = split(q, 2)

    for c in range(3):
        mine = comp == np.float32(c)
        real, imag = (sinus, cosine) if c == 1 else (cosine, -sinus)
        store_q(32 * c, jnp.where(mine, jnp.where(single, 1.0, real), 0.0))
        store_q(128 + 32 * c, jnp.where(mine, jnp.where(single, parity, imag), 0.0))
    store_q(96, jnp.zeros((32, 128), F32))
    store_q(224, jnp.zeros((32, 128), F32))

    total = [jnp.zeros((32, 128), F32) for _ in range(3)]
    for sub in range(2):
        loads[2 * sub].wait()
        loads[2 * sub + 1].wait()
        for z in range(4):
            moment = pick(spc[sub, z] == 1, MOMENT_PAIR)
            v = unit(ang[sub, 0, z], ang[sub, 1, z])
            for c in range(3):
                vec[sub, c, z, 0:32, 0:128] = v[c]
            total = [t + moment * c for t, c in zip(total, v)]
    rows = []
    for c in range(3):
        mom[c] = total[c]
        line = mom[c, pl.ds(0, 8, 4), :]
        for r in range(1, 4):
            line = line + mom[c, pl.ds(r, 8, 4), :]
        rows.append(line)
    atom = iota((384, 128), 0)
    place = ((atom >> 7) << 5) + ((atom & 127) >> 2)
    spread = jnp.where(iota((384, 128), 1) == place, 1 / 128, 0.0).astype(BF16)
    packed = exact_dot(jnp.concatenate(rows, axis=1), spread)
    tile[...] = packed

    pl.semaphore_wait(barrier, nx - 1 + len(near))

    @pl.loop(1, nx)
    def _(o):
        remote(tile, b_a.at[gx], s_a, r_a, (lax.rem(gx + o, nx), gy)).start()

    signal(word.at[0], (gx, at(True, 0)))
    signal(word.at[1], (gx, at(False, -1)))
    signal(word.at[2], (gx, at(True, -1)))

    halo_row, halo_spc, halo_x, halo_c = [
        [remote(src, dst, s_h.at[n], r_h.at[n], to) for src, dst, to in pair]
        for n, pair in enumerate((
            ((ang.at[:, :, :, pl.ds(31, 1), :], g_ang.at[:, :, :, pl.ds(0, 1), :], (gx, above)),
             (ang.at[:, :, :, pl.ds(0, 1), :], g_ang.at[:, :, :, pl.ds(1, 1), :], (gx, below))),
            ((spc.at[:, :, pl.ds(31, 1), :], g_spc.at[:, :, pl.ds(0, 1), :], (gx, above)),
             (spc.at[:, :, pl.ds(0, 1), :], g_spc.at[:, :, pl.ds(1, 1), :], (gx, below))),
            ((pack.at[1], g_x.at[0], (right, gy)), (pack.at[0], g_x.at[1], (left, gy))),
            ((g_x, g_c.at[0], (gx, above)), (g_x, g_c.at[1], (gx, below))),
        ))
    ]
    halo_all = [remote(g, g, s_h.at[n], r_h.at[n], (gx, gy)) for n, g in enumerate((g_ang, g_spc, g_x, g_c))]

    b_a[gx] = packed

    lane = iota((128, 128), 1)
    edges = jnp.zeros((128, 128), F32)
    for q in range(3):
        for sub in range(2):
            n = 2 * q + sub
            block = ang[sub, q] if q < 2 else spc[sub].astype(F32)
            block = block.reshape(128, 128)
            edges = jnp.where(lane == n, pltpu.roll(block, n, 1) if n else block, edges)
            edges = jnp.where(lane == 8 + n, pltpu.roll(block, n + 9, 1), edges)
    edges = jnp.transpose(edges)
    pack[0] = edges[0:8]
    pack[1] = edges[8:16]
    for copy in halo_x + halo_row + halo_spc:
        copy.start()

    def blocks(ref, n, send, recv):
        return remote(ref.at[pl.ds(0, n)], ref.at[pl.ds(0, n)], send, recv, (gx, gy))

    blocks(b_a, nx - 1, s_a, r_a).wait_recv()

    wave = wide_dot(b_a[...].reshape(nx * 8, 128), q_high[...], q_low[...], (1, 1))
    real = jnp.zeros((8, 128), F32)
    imag = jnp.zeros((8, 128), F32)
    for g in range(nx):
        t_re, t_im = wave[8 * g : 8 * g + 8, 0:128], wave[8 * g : 8 * g + 8, 128:256]
        c, s = twist[0, g : g + 1, :], twist[1, g : g + 1, :]
        real = real + (t_re * c + t_im * s)
        imag = imag + (t_im * c - t_re * s)

    lane8 = iota((8, 128), 1)
    is_y = (lane8 >= 32) & (lane8 < 64)
    flip = jnp.where(is_y, np.float32(-1), np.float32(1))
    dn[0] = real * flip
    dn[1] = imag * flip
    for r in range(8):
        up[0, r : r + 1, :] = real[7 - r : 8 - r]
        up[1, r : r + 1, :] = imag[7 - r : 8 - r]

    for n in range(3):
        pl.semaphore_wait(word.at[n], 1)

    @pl.loop(0, chips - 1)
    def _(k):
        slot = chips - 1 - k
        n, a = slot // 2, lax.rem(slot, 2)
        odd = lax.rem(n, 2) == 1
        steps = jnp.where(odd, (n + 1) // 2, nz - n // 2)
        back = jnp.where((n == 0) | (n == nz - 1), n, jnp.where(odd, n + 1, n - 1))
        there = 2 * back + a
        to_chip = nz * jnp.where(a == 1, 1 - side, side) + lax.rem(z_own + steps, nz)
        to = 2 * to_chip + core
        land, mark = b_b.at[core, there], r_b.at[there // group]

        @pl.when(to > gy)
        def _():
            remote(up, land, s_b, mark, (gx, to)).start()

        @pl.when(to < gy)
        def _():
            remote(dn, land, s_b, mark, (gx, to)).start()

    even = core == 0
    b_b[core, 0] = jnp.where(even, up[...], dn[...])

    for load in late_loads:
        load.wait()
    wide = iota((TABLE_ROWS, 128), 1)
    for p in range(2):
        t = tab[p]
        tab2[p] = jnp.where(
            wide < 32,
            pltpu.roll(t, 32, 1),
            jnp.where(wide < 64, -pltpu.roll(t, 64, 1), 0.0),
        )

    halo_all[2].wait_recv()
    for copy in halo_c:
        copy.start()
    halo_all[0].wait_recv()
    halo_all[1].wait_recv()
    halo_all[3].wait_recv()

    cols = jnp.concatenate(
        [g_x[0], g_x[1], g_c[0, 0], g_c[0, 1], g_c[1, 0], g_c[1, 1], jnp.zeros((80, 128), F32)], axis=0
    )
    cols = jnp.transpose(cols)
    lane32 = iota((32, 128), 1)
    rowh = iota((8, 128), 0)
    for q in range(3):
        for sub in range(2):
            n = 2 * q + sub
            for z in range(4):

                def column(piece):
                    part = cols[32 * z : 32 * z + 32, 8 * piece + n : 8 * piece + n + 1]
                    return jnp.broadcast_to(part, (32, 128))

                def spot(piece, y):
                    part = cols[32 * z + y : 32 * z + y + 1, 8 * piece + n : 8 * piece + n + 1]
                    return jnp.broadcast_to(part, (8, 128))

                def edge(side):
                    if q < 2:
                        return jnp.broadcast_to(g_ang[sub, q, z, side : side + 1, :], (8, 128))
                    return jnp.broadcast_to(g_spc[sub, z, side : side + 1, :], (8, 128)).astype(F32)

                if q == 2:
                    raw[n, z, 0:32, 0:128] = spc[sub, z].astype(F32)
                raw[n, z, 0:32, 128:256] = jnp.where(lane32 < 64, column(1), column(0))
                raw[n, z, 32:40, 0:128] = jnp.where(rowh < 4, edge(1), edge(0))
                low = jnp.where(lane8 < 64, spot(3, 31), spot(2, 31))
                high = jnp.where(lane8 < 64, spot(5, 0), spot(4, 0))
                raw[n, z, 32:40, 128:256] = jnp.where(rowh < 4, high, low)

    at_row = iota((40, 256), 0)
    at_col = iota((40, 256), 1)
    y = gy * 32 + jnp.where(at_row < 36, at_row, at_row - 40)
    x = gx * 128 + jnp.where(at_col < 192, at_col, at_col - 256)
    inside = (y >= 0) & (y < ny * 32) & (x >= 0) & (x < nx * 128)
    for sub in range(2):
        for z in range(4):
            for r, l in ((slice(0, 32), slice(128, 256)), (slice(32, 40), slice(0, 256))):
                v = unit(raw[sub, z, r, l], raw[2 + sub, z, r, l])
                for c in range(3):
                    vec[sub, c, z, r, l] = v[c]
            coupling = jnp.where(inside, pick(raw[4 + sub, z] > 0.5, COUPLING_PAIR), 0.0)
            cpl[sub, z] = coupling
            for c in range(3):
                wgt[sub, c, z] = coupling * vec[sub, c, z]

    def neighbours(sub, c, z):
        other = 1 - sub
        near = wgt[other, c, z]
        far = z - 1 if sub == 0 else z + 1
        if 0 <= far < 4:
            near = near + wgt[other, c, far]
        near = near + pltpu.roll(near, 1 if sub == 0 else 255, 1)
        return near + pltpu.roll(near, 1 if sub == 0 else 39, 0)

    ratio_pair = [np.float32(EXCHANGE_SCALE) * np.float32(r) for r in RATIO_PAIR]
    for sub in range(2):
        for z in range(4):
            cobalt = raw[4 + sub, z] > 0.5
            ratio = pick(cobalt, ratio_pair)
            for c in range(3):
                h = ratio * neighbours(sub, c, z)
                if c == 2:
                    h = h + pick(cobalt, EASY_PAIR) * vec[sub, c, z]
                fix[sub, c, z] = h

    def hand_on(g):
        part = b_b.at[core, pl.ds(group * g, group)]
        return remote(part, part, s_f.at[g], r_f.at[g], (gx, partner))

    for g in range(GROUPS):
        blocks(b_b.at[core], group - (g == 0), s_b, r_b.at[g]).wait_recv()
        hand_on(g).start()

    zero = jnp.zeros((8, 128), F32)

    def swapped(s):
        return jnp.where(lane8 < 32, pltpu.roll(s, 96, 1), pltpu.roll(s, 32, 1))

    def add_source(d, parts, acc):
        acc = list(acc)
        for p in range(2):
            s = parts[p]
            t = swapped(s)
            for w in range(WINDOWS):
                span = pl.ds(8 * d + w, 8)
                acc[2 * w + p] = acc[2 * w + p] + tab[p, span, :] * s + tab2[p, span, :] * t
        acc[-1] = acc[-1] + parts[1]
        return tuple(acc)

    def add_chips(which, acc_up, acc_dn):
        def source(k):
            ahead = lax.rem(lax.rem(k, nz) - z_own + nz, nz)
            n = jnp.where(
                ahead == 0, 0, jnp.where(ahead <= hops, 2 * ahead - 1, 2 * (nz - ahead))
            )
            slot = 2 * n + jnp.where(k // nz == side, 0, 1)
            return b_b[which, slot, 0], b_b[which, slot, 1]

        acc_up = lax.fori_loop(
            0, chip, lambda k, a: add_source(gy - (2 * k + which), source(k), a), acc_up
        )
        acc_dn = lax.fori_loop(
            chip + 1, chips, lambda k, a: add_source(2 * k + which - gy, source(k), a), acc_dn
        )
        return acc_up, acc_dn

    start = tuple(zero for _ in range(2 * WINDOWS + 1))
    acc_up = add_source(0, (up[0], up[1]), start)
    acc_up, acc_dn = add_chips(core, acc_up, start)
    for g in range(GROUPS):
        hand_on(g).wait_recv()
    acc_up, acc_dn = add_chips(1 - core, acc_up, acc_dn)
    beside = (b_b[1 - core, 0, 0], b_b[1 - core, 0, 1])
    acc_up = lax.fori_loop(0, core, lambda _, a: add_source(1, beside, a), acc_up)
    acc_dn = lax.fori_loop(0, 1 - core, lambda _, a: add_source(1, beside, a), acc_dn)

    alternate = jnp.where(iota((8, 128), 0) % 2 == 0, np.float32(1), np.float32(-1))
    last = jnp.sum((flip * acc_dn[-1] - acc_up[-1]) * alternate, axis=0, keepdims=True)
    last = jnp.broadcast_to(last, (8, 128))
    last = swapped(last)
    last = jnp.where(((lane8 == 0) | (lane8 == 32)) & (gx == 0), last, 0.0) * np.float32(corner)

    row16 = iota((16, 128), 0)
    field = []
    for p in range(2):
        out = jnp.zeros((16, 128), F32)
        for w in range(WINDOWS):
            sums = acc_up[2 * w + p] + flip * acc_dn[2 * (WINDOWS - 1 - w) + p]
            if p == 1:
                sign = np.float32((1 if w % 2 else -1) / 8)
                sums = sums + sign * last
            line = jnp.sum(sums, axis=0, keepdims=True)
            out = jnp.where(row16 == w, jnp.broadcast_to(line, (16, 128)), out)
        field.append(out)

    turned = []
    for g in range(nx):
        c, s = twist[0, g : g + 1, :], twist[1, g : g + 1, :]
        turned.append(
            jnp.concatenate([field[0] * c - field[1] * s, field[0] * s + field[1] * c], axis=1)
        )
    shares = wide_dot(jnp.concatenate(turned, axis=0), q_high[...], q_low[...], (1, 0))
    send_c[...] = shares.reshape(nx, 16, 128)

    @pl.loop(1, nx)
    def _(o):
        to = lax.rem(gx + o, nx)
        part = pl.ds(0, WINDOWS)
        remote(send_c.at[to, part], b_c.at[gx, part], s_c, r_c, (to, gy)).start()

    b_c[gx] = send_c[gx]
    atom = iota((128, 256), 1)
    want = jnp.where(atom < 128, atom >> 2, jnp.where(atom < 192, 97, 96))
    scale = jnp.where(atom < 128, 32, 2)
    hot = [
        jnp.where(iota((128, 256), 0) == want + scale * c, 1.0, 0.0).astype(BF16) for c in range(3)
    ]
    row8 = iota((8, 256), 0)

    all_c = b_c.at[pl.ds(0, nx - 1), pl.ds(0, WINDOWS)]
    shares_in = remote(all_c, all_c, s_c, r_c, (gx, gy))
    shares_in.wait_recv()
    whole = b_c[0]
    for g in range(1, nx):
        whole = whole + b_c[g]

    fld[...] = whole
    for c in range(3):
        lines = exact_dot(whole, hot[c])

        def line(w):
            return jnp.broadcast_to(lines[w : w + 1], (8, 256))

        for t in range(4):
            dpl[c, pl.ds(8 * t, 8), :] = jnp.where(row8 < 4, line(2 * t + 1), line(2 * t + 2))
        dpl[c, pl.ds(32, 8), :] = jnp.where(row8 < 4, line(9), line(0))

    for sub in range(2):
        for z in range(4):
            v = [vec[sub, c, z] for c in range(3)]
            f = torque(v, [fix[sub, c, z] + dpl[c] for c in range(3)])
            p = normalized([a + np.float32(TIME_STEP) * b for a, b in zip(v, f)])
            coupling = cpl[sub, z]
            for c in range(3):
                wgt[sub, c, z] = coupling * p[c]
                fix[sub, c, z, 0:32, 0:128] = p[c][0:32, 0:128]
                nxt[sub, c, z] = f[c][0:32, 0:128]
    for sub in range(2):
        for z in range(4):
            cobalt = spc[sub, z] == 1
            ratio = pick(cobalt, ratio_pair)
            p = [fix[sub, c, z, 0:32, 0:128] for c in range(3)]
            h = [
                ratio * neighbours(sub, c, z)[0:32, 0:128] + dpl[c, 0:32, 0:128] for c in range(3)
            ]
            h[2] = h[2] + pick(cobalt, EASY_PAIR) * p[2]
            f = torque(p, h)
            w = [
                vec[sub, c, z, 0:32, 0:128] + np.float32(0.5 * TIME_STEP) * (nxt[sub, c, z] + f[c])
                for c in range(3)
            ]
            for c in range(3):
                nxt[sub, c, z] = w[c]

    for halo in halo_all:
        halo.wait_send()
    blocks(b_a, nx - 1, s_a, r_a).wait_send()
    shares_in.wait_send()
    blocks(b_b.at[core], chips - 1, s_b, r_b.at[0]).wait_send()
    for g in range(GROUPS):
        hand_on(g).wait_send()


def finish_kernel(raw, fld, nxt, dip):
    for c in range(3):
        dip[c, 0] = fld[1:9, 32 * c : 32 * c + 32]
    for sub in range(2):
        for z in range(4):
            w = normalized([raw[sub, c, z] for c in range(3)])
            for c in range(3):
                nxt[sub, c, z] = w[c]


def solution(mesh):
    nx, ny = mesh.shape["gx"], mesh.shape["gy"]
    table, corner = wave_tables(nx, ny)
    base, phase, twist, lanes = trig_tables(nx)
    vmem = pl.BlockSpec(memory_space=pltpu.VMEM)
    hbm = pl.BlockSpec(memory_space=pl.ANY)
    dma = pltpu.SemaphoreType.DMA
    regular = pltpu.SemaphoreType.REGULAR

    def scratch(*shape, dtype=F32):
        return pltpu.VMEM(shape, dtype)

    def on_device(spin_angles, species):
        raw, fld = pl.pallas_call(
            functools.partial(step_kernel, nx, ny, corner),
            out_shape=[
                jax.ShapeDtypeStruct((2, 3, 4, 32, 128), F32),
                jax.ShapeDtypeStruct((16, 128), F32),
            ],
            in_specs=[hbm] * 7,
            out_specs=[vmem] * 2,
            scratch_shapes=[
                scratch(2, PART_K, 128),
                scratch(2, 128),
                scratch(2, nx, 128),
                scratch(2, 128),
                scratch(2, 2, 4, 32, 128),
                scratch(2, 4, 32, 128, dtype=jnp.int32),
                scratch(3, 32, 128),
                scratch(8, 128),
                scratch(nx, 8, 128),
                scratch(256, 128, dtype=BF16),
                scratch(256, 128, dtype=BF16),
                scratch(2, TABLE_ROWS, 128),
                scratch(2, TABLE_ROWS, 128),
                scratch(2, 8, 128),
                scratch(2, 8, 128),
                scratch(2, ny // 2, 2, 8, 128),
                scratch(nx, 16, 128),
                scratch(nx, 16, 128),
                scratch(2, 8, 128),
                scratch(2, 2, 4, 2, 128),
                scratch(2, 4, 2, 128, dtype=jnp.int32),
                scratch(2, 8, 128),
                scratch(2, 2, 8, 128),
                scratch(6, 4, 40, 256),
                scratch(2, 4, 40, 256),
                scratch(2, 3, 4, 40, 256),
                scratch(2, 3, 4, 40, 256),
                scratch(2, 3, 4, 40, 256),
                scratch(3, 40, 256),
                dma((10,)),
                dma, dma, dma, dma((GROUPS,)), dma((GROUPS,)), dma((GROUPS,)), dma, dma,
                dma((4,)),
                dma((4,)),
                regular((3,)),
            ],
            compiler_params=pltpu.CompilerParams(collective_id=0, has_side_effects=True),
        )(spin_angles, species, table, base, phase, twist, lanes)
        return pl.pallas_call(
            finish_kernel,
            out_shape=[
                jax.ShapeDtypeStruct((2, 3, 4, 32, 128), F32),
                jax.ShapeDtypeStruct((3, 1, 8, 32), F32),
            ],
            in_specs=[vmem] * 2,
            out_specs=[vmem] * 2,
        )(raw, fld)

    return jax.shard_map(
        lambda a, s: tuple(on_device(a, s)),
        mesh=mesh,
        in_specs=(P(None, None, None, "gy", "gx"), P(None, None, "gy", "gx")),
        out_specs=(P(None, None, None, "gy", "gx"), P(None, None, "gy", "gx")),
        check_vma=False,
    )
```

```python
import functools
import math

import jax
import jax.numpy as jnp
import numpy as np
from jax import lax
from jax.experimental import pallas as pl
from jax.experimental.pallas import tpu as pltpu
from jax.sharding import PartitionSpec as P

MESH = pl.DeviceIdType.MESH
F32, BF16 = jnp.float32, jnp.bfloat16

CELLS_M = 4
DAMPING = 0.1
TIME_STEP = 0.05
EXCHANGE_SCALE = 0.6
DIPOLE = 2.0
MOMENT_PAIR = (2.22, 1.72)
COUPLING_PAIR = (1.0, 1.25)
ANISOTROPY_PAIR = (0.3, 0.9)
RATIO_PAIR = (COUPLING_PAIR[0] / MOMENT_PAIR[0], COUPLING_PAIR[1] / MOMENT_PAIR[1])
EASY_PAIR = (2 * ANISOTROPY_PAIR[0] / MOMENT_PAIR[0], 2 * ANISOTROPY_PAIR[1] / MOMENT_PAIR[1])

PART_K = 32
ROWS = 8
COLS = 32
GROUPS = 6
WINDOWS = 10
TABLE_LEAD = 8
TABLE_ROWS = 400


def wave_tables(nx, ny):
    period_x, period_y = 2 * nx * COLS, 2 * ny * ROWS
    half_y = period_y // 2
    v = np.arange(period_x // 2 + 1)
    u = np.arange(half_y + 1)
    a = 2 * np.pi * v[:, None] / period_x
    b = 2 * np.pi * u[None, :] / period_y
    k = np.sqrt(a * a + b * b)
    inv = np.where(k > 0, 1.0 / np.where(k > 0, k, 1.0), 0.0)
    g = {
        "xx": -a * a * 0.5 * inv,
        "yy": -b * b * 0.5 * inv,
        "zz": 0.5 * k - 1.0,
        "xy": -a * b * 0.5 * inv,
    }
    dy = np.arange(-TABLE_LEAD, TABLE_ROWS - TABLE_LEAD)
    angle = 2 * np.pi * ((u[:, None] * dy[None, :]) % period_y) / period_y
    fold = np.where((u == 0) | (u == half_y), 1.0, 2.0)
    cosine = fold[:, None] * np.cos(angle)
    sine = np.where((u == 0) | (u == half_y), 0.0, 2.0)[:, None] * np.sin(angle)
    scale = DIPOLE / (period_x * period_y) * np.where((v == 0) | (v == period_x // 2), 1.0, 2.0)
    tables = [scale[:, None] * (g[n] @ cosine) for n in ("xx", "yy", "zz")]
    odd = scale[:, None] * (g["xy"] @ sine)
    odd[-1] = 0.0
    tables.append(odd)
    lanes = np.stack(tables)
    out = np.zeros((nx + 1, TABLE_ROWS, 4 * PART_K), np.float32)
    for s in range(nx):
        block = lanes[:, s * PART_K : (s + 1) * PART_K, :]
        out[s] = block.transpose(2, 0, 1).reshape(TABLE_ROWS, -1)
    out[nx] = out[0]
    for n in range(4):
        out[nx, :, n * PART_K] = lanes[n, -1, :]
    corner = DIPOLE / (period_x * period_y) * float(-0.5 * np.pi * np.pi / np.sqrt(2 * np.pi**2))
    return out, corner


def trig_tables(nx):
    period = 2 * nx * COLS
    lane = np.arange(128)
    comp = np.where(lane < 96, lane // 32, np.where(lane < 102, (lane - 96) // 2, 3))
    place = np.where(lane < 96, lane % 32, np.where(lane % 2 == 0, -1, 32))
    j = np.arange(PART_K)
    t = 2 * np.pi * ((j[:, None] * place[None, :]) % period) / period
    base = np.stack([np.cos(t), np.sin(t)]).astype(np.float32)
    s = np.arange(nx)
    t = 2 * np.pi * ((s[:, None] * PART_K * place[None, :]) % period) / period
    phase = np.stack([np.cos(t), np.sin(t)], axis=1).astype(np.float32)
    jl = lane % 32
    t = 2 * np.pi * ((s[:, None] * COLS * jl[None, :]) % period) / period
    twist = np.stack([np.cos(t), np.sin(t)]).astype(np.float32)
    row = np.stack([comp, np.where(place % 2 == 0, 1, -1)]).astype(np.float32)
    return base, phase, twist, row


def sine(r):
    q = r * r
    p = 1.0 / 6227020800.0
    for c in (-1.0 / 39916800.0, 1.0 / 362880.0, -1.0 / 5040.0, 1.0 / 120.0, -1.0 / 6.0):
        p = p * q + c
    return r + r * q * p


def sine_cosine(x):
    size = jnp.abs(x)
    far = (np.float32(math.pi) - size) + np.float32(math.pi - float(np.float32(math.pi)))
    s = sine(jnp.where(size > np.float32(math.pi / 2), far, size))
    half = (np.float32(math.pi / 2) - size) + np.float32(
        math.pi / 2 - float(np.float32(math.pi / 2))
    )
    return jnp.where(x < 0, -s, s), sine(half)


def pick(cobalt, pair):
    return jnp.where(cobalt, np.float32(pair[1]), np.float32(pair[0]))


def unit(polar, azimuth):
    sp, cp = sine_cosine(polar)
    sq, cq = sine_cosine(azimuth)
    return sp * cq, sp * sq, cp


def iota(shape, dim):
    return lax.broadcasted_iota(jnp.int32, shape, dim)


def cross(a, b):
    return (
        a[1] * b[2] - a[2] * b[1],
        a[2] * b[0] - a[0] * b[2],
        a[0] * b[1] - a[1] * b[0],
    )


def torque(v, h):
    p = cross(v, h)
    r = cross(v, p)
    return [
        (a + np.float32(DAMPING) * b) * np.float32(-1.0 / (1.0 + DAMPING * DAMPING))
        for a, b in zip(p, r)
    ]


def normalized(w):
    s = w[0] * w[0] + w[1] * w[1] + w[2] * w[2]
    r = lax.rsqrt(s)
    r = r * (1.5 - 0.5 * s * r * r)
    return [c * r for c in w]


def split(x, pieces):
    out = []
    for _ in range(pieces):
        out.append(x.astype(BF16))
        x = x - out[-1].astype(F32)
    return out


def dot(a, b, dims=(1, 0)):
    return lax.dot_general(
        a, b, (((dims[0],), (dims[1],)), ((), ())), preferred_element_type=F32
    )


def exact_dot(a, hot):
    n = a.shape[0]
    out = dot(jnp.concatenate(split(a, 3), axis=0), hot)
    return out[0:n] + out[n : 2 * n] + out[2 * n : 3 * n]


def wide_dot(a, b_high, b_low, dims):
    n = a.shape[0]
    high, low = split(a, 2)
    out = dot(jnp.concatenate([high, low], axis=0), b_high, dims)
    return out[0:n] + out[n : 2 * n] + dot(high, b_low, dims)


def step_kernel(
    nx, ny, corner,
    ang_hbm, spc_hbm, table_hbm, base_hbm, phase_hbm, twist_hbm, lanes_hbm,
    nxt, fld,
    base, phase, twist, lanes, ang, spc, mom, tile, b_a, q_high, q_low, tab, tab2, up, dn, b_b, send_c, b_c, pack, g_ang, g_spc, g_x, g_c,
    raw, cpl, vec, wgt, fix, dpl,
    load_sem, s_a, r_a, s_b, r_b, s_f, r_f, s_c, r_c, s_h, r_h, word,
):
    gx, gy = lax.axis_index("gx"), lax.axis_index("gy")
    left, right = lax.rem(gx + nx - 1, nx), lax.rem(gx + 1, nx)
    below, above = lax.rem(gy + ny - 1, ny), lax.rem(gy + 1, ny)
    core = lax.rem(gy, 2)
    chip = gy // 2
    partner = gy + 1 - 2 * core
    chips = ny // 2
    nz = ny // 4
    hops = nz // 2
    side, z_own = chip // nz, lax.rem(chip, nz)

    def at(across, dz):
        there = (1 - side) if across else side
        return 2 * (nz * there + lax.rem(z_own + dz + nz, nz)) + core

    group = chips // GROUPS

    loads = []
    for sub in range(2):
        loads.append(pltpu.make_async_copy(ang_hbm.at[sub], ang.at[sub], load_sem.at[2 * sub]))
        loads.append(pltpu.make_async_copy(spc_hbm.at[sub], spc.at[sub], load_sem.at[2 * sub + 1]))
    late_loads = [
        pltpu.make_async_copy(table_hbm.at[gx], tab.at[0], load_sem.at[4]),
        pltpu.make_async_copy(table_hbm.at[jnp.where(gx == 0, nx, gx)], tab.at[1], load_sem.at[5]),
    ]
    small_loads = [
        pltpu.make_async_copy(src, dst, load_sem.at[6 + n])
        for n, (src, dst) in enumerate(
            ((base_hbm, base), (phase_hbm.at[gx], phase), (lanes_hbm, lanes), (twist_hbm, twist))
        )
    ]
    for load in small_loads + loads + late_loads:
        load.start()

    barrier = pltpu.get_barrier_semaphore()

    def signal(semaphore, device):
        pl.semaphore_signal(semaphore, inc=1, device_id=device, device_id_type=MESH)

    @pl.loop(1, nx)
    def _(o):
        signal(barrier, (lax.rem(gx + o, nx), gy))

    near = [above, below, at(True, 0), at(True, 1), at(True, -1)]
    for dz in range(1, hops):
        near += [at(False, dz), at(False, -dz)]
    for other in near:
        signal(barrier, (gx, other))

    def remote(src, dst, send, recv, device):
        return pltpu.make_async_remote_copy(
            src_ref=src, dst_ref=dst, send_sem=send, recv_sem=recv, device_id=device, device_id_type=MESH
        )

    for load in small_loads:
        load.wait()
    b_cos, b_sin = base[0], base[1]
    p_cos, p_sin = phase[0:1, :], phase[1:2, :]
    cosine = b_cos * p_cos - b_sin * p_sin
    sinus = b_sin * p_cos + b_cos * p_sin
    comp, parity = lanes[0:1, :], lanes[1:2, :]
    single = (iota((32, 128), 0) + gx) == 0

    def store_q(at, q):
        q_high[pl.ds(at, 32), :], q_low[pl.ds(at, 32), :] = split(q, 2)

    for c in range(3):
        mine = comp == np.float32(c)
        real, imag = (sinus, cosine) if c == 1 else (cosine, -sinus)
        store_q(32 * c, jnp.where(mine, jnp.where(single, 1.0, real), 0.0))
        store_q(128 + 32 * c, jnp.where(mine, jnp.where(single, parity, imag), 0.0))
    store_q(96, jnp.zeros((32, 128), F32))
    store_q(224, jnp.zeros((32, 128), F32))

    total = [jnp.zeros((32, 128), F32) for _ in range(3)]
    for sub in range(2):
        loads[2 * sub].wait()
        loads[2 * sub + 1].wait()
        for z in range(4):
            moment = pick(spc[sub, z] == 1, MOMENT_PAIR)
            v = unit(ang[sub, 0, z], ang[sub, 1, z])
            for c in range(3):
                vec[sub, c, z, 0:32, 0:128] = v[c]
            total = [t + moment * c for t, c in zip(total, v)]
    rows = []
    for c in range(3):
        mom[c] = total[c]
        line = mom[c, pl.ds(0, 8, 4), :]
        for r in range(1, 4):
            line = line + mom[c, pl.ds(r, 8, 4), :]
        rows.append(line)
    atom = iota((384, 128), 0)
    place = ((atom >> 7) << 5) + ((atom & 127) >> 2)
    spread = jnp.where(iota((384, 128), 1) == place, 1 / 128, 0.0).astype(BF16)
    packed = exact_dot(jnp.concatenate(rows, axis=1), spread)
    tile[...] = packed

    pl.semaphore_wait(barrier, nx - 1 + len(near))

    @pl.loop(1, nx)
    def _(o):
        remote(tile, b_a.at[gx], s_a, r_a, (lax.rem(gx + o, nx), gy)).start()

    signal(word.at[0], (gx, at(True, 0)))
    signal(word.at[1], (gx, at(False, -1)))
    signal(word.at[2], (gx, at(True, -1)))

    halo_row, halo_spc, halo_x, halo_c = [
        [remote(src, dst, s_h.at[n], r_h.at[n], to) for src, dst, to in pair]
        for n, pair in enumerate((
            ((ang.at[:, :, :, pl.ds(31, 1), :], g_ang.at[:, :, :, pl.ds(0, 1), :], (gx, above)),
             (ang.at[:, :, :, pl.ds(0, 1), :], g_ang.at[:, :, :, pl.ds(1, 1), :], (gx, below))),
            ((spc.at[:, :, pl.ds(31, 1), :], g_spc.at[:, :, pl.ds(0, 1), :], (gx, above)),
             (spc.at[:, :, pl.ds(0, 1), :], g_spc.at[:, :, pl.ds(1, 1), :], (gx, below))),
            ((pack.at[1], g_x.at[0], (right, gy)), (pack.at[0], g_x.at[1], (left, gy))),
            ((g_x, g_c.at[0], (gx, above)), (g_x, g_c.at[1], (gx, below))),
        ))
    ]
    halo_all = [remote(g, g, s_h.at[n], r_h.at[n], (gx, gy)) for n, g in enumerate((g_ang, g_spc, g_x, g_c))]

    b_a[gx] = packed

    lane = iota((128, 128), 1)
    edges = jnp.zeros((128, 128), F32)
    for q in range(3):
        for sub in range(2):
            n = 2 * q + sub
            block = ang[sub, q] if q < 2 else spc[sub].astype(F32)
            block = block.reshape(128, 128)
            edges = jnp.where(lane == n, pltpu.roll(block, n, 1) if n else block, edges)
            edges = jnp.where(lane == 8 + n, pltpu.roll(block, n + 9, 1), edges)
    edges = jnp.transpose(edges)
    pack[0] = edges[0:8]
    pack[1] = edges[8:16]
    for copy in halo_x + halo_row + halo_spc:
        copy.start()

    def blocks(ref, n, send, recv):
        return remote(ref.at[pl.ds(0, n)], ref.at[pl.ds(0, n)], send, recv, (gx, gy))

    blocks(b_a, nx - 1, s_a, r_a).wait_recv()

    wave = wide_dot(b_a[...].reshape(nx * 8, 128), q_high[...], q_low[...], (1, 1))
    real = jnp.zeros((8, 128), F32)
    imag = jnp.zeros((8, 128), F32)
    for g in range(nx):
        t_re, t_im = wave[8 * g : 8 * g + 8, 0:128], wave[8 * g : 8 * g + 8, 128:256]
        c, s = twist[0, g : g + 1, :], twist[1, g : g + 1, :]
        real = real + (t_re * c + t_im * s)
        imag = imag + (t_im * c - t_re * s)

    lane8 = iota((8, 128), 1)
    is_y = (lane8 >= 32) & (lane8 < 64)
    flip = jnp.where(is_y, np.float32(-1), np.float32(1))
    dn[0] = real * flip
    dn[1] = imag * flip
    for r in range(8):
        up[0, r : r + 1, :] = real[7 - r : 8 - r]
        up[1, r : r + 1, :] = imag[7 - r : 8 - r]

    for n in range(3):
        pl.semaphore_wait(word.at[n], 1)

    @pl.loop(0, chips - 1)
    def _(k):
        slot = chips - 1 - k
        n, a = slot // 2, lax.rem(slot, 2)
        odd = lax.rem(n, 2) == 1
        steps = jnp.where(odd, (n + 1) // 2, nz - n // 2)
        back = jnp.where((n == 0) | (n == nz - 1), n, jnp.where(odd, n + 1, n - 1))
        there = 2 * back + a
        to_chip = nz * jnp.where(a == 1, 1 - side, side) + lax.rem(z_own + steps, nz)
        to = 2 * to_chip + core
        land, mark = b_b.at[core, there], r_b.at[there // group]

        @pl.when(to > gy)
        def _():
            remote(up, land, s_b, mark, (gx, to)).start()

        @pl.when(to < gy)
        def _():
            remote(dn, land, s_b, mark, (gx, to)).start()

    even = core == 0
    b_b[core, 0] = jnp.where(even, up[...], dn[...])

    for load in late_loads:
        load.wait()
    wide = iota((TABLE_ROWS, 128), 1)
    for p in range(2):
        t = tab[p]
        tab2[p] = jnp.where(
            wide < 32,
            pltpu.roll(t, 32, 1),
            jnp.where(wide < 64, -pltpu.roll(t, 64, 1), 0.0),
        )

    halo_all[2].wait_recv()
    for copy in halo_c:
        copy.start()
    halo_all[0].wait_recv()
    halo_all[1].wait_recv()
    halo_all[3].wait_recv()

    cols = jnp.concatenate(
        [g_x[0], g_x[1], g_c[0, 0], g_c[0, 1], g_c[1, 0], g_c[1, 1], jnp.zeros((80, 128), F32)], axis=0
    )
    cols = jnp.transpose(cols)
    lane32 = iota((32, 128), 1)
    rowh = iota((8, 128), 0)
    for q in range(3):
        for sub in range(2):
            n = 2 * q + sub
            for z in range(4):

                def column(piece):
                    part = cols[32 * z : 32 * z + 32, 8 * piece + n : 8 * piece + n + 1]
                    return jnp.broadcast_to(part, (32, 128))

                def spot(piece, y):
                    part = cols[32 * z + y : 32 * z + y + 1, 8 * piece + n : 8 * piece + n + 1]
                    return jnp.broadcast_to(part, (8, 128))

                def edge(side):
                    if q < 2:
                        return jnp.broadcast_to(g_ang[sub, q, z, side : side + 1, :], (8, 128))
                    return jnp.broadcast_to(g_spc[sub, z, side : side + 1, :], (8, 128)).astype(F32)

                if q == 2:
                    raw[n, z, 0:32, 0:128] = spc[sub, z].astype(F32)
                raw[n, z, 0:32, 128:256] = jnp.where(lane32 < 64, column(1), column(0))
                raw[n, z, 32:40, 0:128] = jnp.where(rowh < 4, edge(1), edge(0))
                low = jnp.where(lane8 < 64, spot(3, 31), spot(2, 31))
                high = jnp.where(lane8 < 64, spot(5, 0), spot(4, 0))
                raw[n, z, 32:40, 128:256] = jnp.where(rowh < 4, high, low)

    at_row = iota((40, 256), 0)
    at_col = iota((40, 256), 1)
    y = gy * 32 + jnp.where(at_row < 36, at_row, at_row - 40)
    x = gx * 128 + jnp.where(at_col < 192, at_col, at_col - 256)
    inside = (y >= 0) & (y < ny * 32) & (x >= 0) & (x < nx * 128)
    for sub in range(2):
        for z in range(4):
            for r, l in ((slice(0, 32), slice(128, 256)), (slice(32, 40), slice(0, 256))):
                v = unit(raw[sub, z, r, l], raw[2 + sub, z, r, l])
                for c in range(3):
                    vec[sub, c, z, r, l] = v[c]
            coupling = jnp.where(inside, pick(raw[4 + sub, z] > 0.5, COUPLING_PAIR), 0.0)
            cpl[sub, z] = coupling
            for c in range(3):
                wgt[sub, c, z] = coupling * vec[sub, c, z]

    def neighbours(sub, c, z):
        other = 1 - sub
        near = wgt[other, c, z]
        far = z - 1 if sub == 0 else z + 1
        if 0 <= far < 4:
            near = near + wgt[other, c, far]
        near = near + pltpu.roll(near, 1 if sub == 0 else 255, 1)
        return near + pltpu.roll(near, 1 if sub == 0 else 39, 0)

    ratio_pair = [np.float32(EXCHANGE_SCALE) * np.float32(r) for r in RATIO_PAIR]
    for sub in range(2):
        for z in range(4):
            cobalt = raw[4 + sub, z] > 0.5
            ratio = pick(cobalt, ratio_pair)
            for c in range(3):
                h = ratio * neighbours(sub, c, z)
                if c == 2:
                    h = h + pick(cobalt, EASY_PAIR) * vec[sub, c, z]
                fix[sub, c, z] = h

    def hand_on(g):
        part = b_b.at[core, pl.ds(group * g, group)]
        return remote(part, part, s_f.at[g], r_f.at[g], (gx, partner))

    for g in range(GROUPS):
        blocks(b_b.at[core], group - (g == 0), s_b, r_b.at[g]).wait_recv()
        hand_on(g).start()

    zero = jnp.zeros((8, 128), F32)

    def swapped(s):
        return jnp.where(lane8 < 32, pltpu.roll(s, 96, 1), pltpu.roll(s, 32, 1))

    def add_source(d, parts, acc):
        acc = list(acc)
        for p in range(2):
            s = parts[p]
            t = swapped(s)
            for w in range(WINDOWS):
                span = pl.ds(8 * d + w, 8)
                acc[2 * w + p] = acc[2 * w + p] + tab[p, span, :] * s + tab2[p, span, :] * t
        acc[-1] = acc[-1] + parts[1]
        return tuple(acc)

    def add_chips(which, acc_up, acc_dn):
        def source(k):
            ahead = lax.rem(lax.rem(k, nz) - z_own + nz, nz)
            n = jnp.where(
                ahead == 0, 0, jnp.where(ahead <= hops, 2 * ahead - 1, 2 * (nz - ahead))
            )
            slot = 2 * n + jnp.where(k // nz == side, 0, 1)
            return b_b[which, slot, 0], b_b[which, slot, 1]

        acc_up = lax.fori_loop(
            0, chip, lambda k, a: add_source(gy - (2 * k + which), source(k), a), acc_up
        )
        acc_dn = lax.fori_loop(
            chip + 1, chips, lambda k, a: add_source(2 * k + which - gy, source(k), a), acc_dn
        )
        return acc_up, acc_dn

    start = tuple(zero for _ in range(2 * WINDOWS + 1))
    acc_up = add_source(0, (up[0], up[1]), start)
    acc_up, acc_dn = add_chips(core, acc_up, start)
    for g in range(GROUPS):
        hand_on(g).wait_recv()
    acc_up, acc_dn = add_chips(1 - core, acc_up, acc_dn)
    beside = (b_b[1 - core, 0, 0], b_b[1 - core, 0, 1])
    acc_up = lax.fori_loop(0, core, lambda _, a: add_source(1, beside, a), acc_up)
    acc_dn = lax.fori_loop(0, 1 - core, lambda _, a: add_source(1, beside, a), acc_dn)

    alternate = jnp.where(iota((8, 128), 0) % 2 == 0, np.float32(1), np.float32(-1))
    last = jnp.sum((flip * acc_dn[-1] - acc_up[-1]) * alternate, axis=0, keepdims=True)
    last = jnp.broadcast_to(last, (8, 128))
    last = swapped(last)
    last = jnp.where(((lane8 == 0) | (lane8 == 32)) & (gx == 0), last, 0.0) * np.float32(corner)

    row16 = iota((16, 128), 0)
    field = []
    for p in range(2):
        out = jnp.zeros((16, 128), F32)
        for w in range(WINDOWS):
            sums = acc_up[2 * w + p] + flip * acc_dn[2 * (WINDOWS - 1 - w) + p]
            if p == 1:
                sign = np.float32((1 if w % 2 else -1) / 8)
                sums = sums + sign * last
            line = jnp.sum(sums, axis=0, keepdims=True)
            out = jnp.where(row16 == w, jnp.broadcast_to(line, (16, 128)), out)
        field.append(out)

    turned = []
    for g in range(nx):
        c, s = twist[0, g : g + 1, :], twist[1, g : g + 1, :]
        turned.append(
            jnp.concatenate([field[0] * c - field[1] * s, field[0] * s + field[1] * c], axis=1)
        )
    shares = wide_dot(jnp.concatenate(turned, axis=0), q_high[...], q_low[...], (1, 0))
    send_c[...] = shares.reshape(nx, 16, 128)

    @pl.loop(1, nx)
    def _(o):
        to = lax.rem(gx + o, nx)
        part = pl.ds(0, WINDOWS)
        remote(send_c.at[to, part], b_c.at[gx, part], s_c, r_c, (to, gy)).start()

    b_c[gx] = send_c[gx]
    atom = iota((128, 256), 1)
    want = jnp.where(atom < 128, atom >> 2, jnp.where(atom < 192, 97, 96))
    scale = jnp.where(atom < 128, 32, 2)
    hot = [
        jnp.where(iota((128, 256), 0) == want + scale * c, 1.0, 0.0).astype(BF16) for c in range(3)
    ]
    row8 = iota((8, 256), 0)

    all_c = b_c.at[pl.ds(0, nx - 1), pl.ds(0, WINDOWS)]
    shares_in = remote(all_c, all_c, s_c, r_c, (gx, gy))
    shares_in.wait_recv()
    whole = b_c[0]
    for g in range(1, nx):
        whole = whole + b_c[g]

    fld[...] = whole
    for c in range(3):
        lines = exact_dot(whole, hot[c])

        def line(w):
            return jnp.broadcast_to(lines[w : w + 1], (8, 256))

        for t in range(4):
            dpl[c, pl.ds(8 * t, 8), :] = jnp.where(row8 < 4, line(2 * t + 1), line(2 * t + 2))
        dpl[c, pl.ds(32, 8), :] = jnp.where(row8 < 4, line(9), line(0))

    for sub in range(2):
        for z in range(4):
            v = [vec[sub, c, z] for c in range(3)]
            f = torque(v, [fix[sub, c, z] + dpl[c] for c in range(3)])
            p = normalized([a + np.float32(TIME_STEP) * b for a, b in zip(v, f)])
            coupling = cpl[sub, z]
            for c in range(3):
                wgt[sub, c, z] = coupling * p[c]
                fix[sub, c, z, 0:32, 0:128] = p[c][0:32, 0:128]
                nxt[sub, c, z] = f[c][0:32, 0:128]
    for sub in range(2):
        for z in range(4):
            cobalt = spc[sub, z] == 1
            ratio = pick(cobalt, ratio_pair)
            p = [fix[sub, c, z, 0:32, 0:128] for c in range(3)]
            h = [
                ratio * neighbours(sub, c, z)[0:32, 0:128] + dpl[c, 0:32, 0:128] for c in range(3)
            ]
            h[2] = h[2] + pick(cobalt, EASY_PAIR) * p[2]
            f = torque(p, h)
            w = [
                vec[sub, c, z, 0:32, 0:128] + np.float32(0.5 * TIME_STEP) * (nxt[sub, c, z] + f[c])
                for c in range(3)
            ]
            for c in range(3):
                nxt[sub, c, z] = w[c]

    for halo in halo_all:
        halo.wait_send()
    blocks(b_a, nx - 1, s_a, r_a).wait_send()
    shares_in.wait_send()
    blocks(b_b.at[core], chips - 1, s_b, r_b.at[0]).wait_send()
    for g in range(GROUPS):
        hand_on(g).wait_send()


def finish_kernel(raw, fld, nxt, dip):
    for c in range(3):
        dip[c, 0] = fld[1:9, 32 * c : 32 * c + 32]
    for sub in range(2):
        for z in range(4):
            w = normalized([raw[sub, c, z] for c in range(3)])
            for c in range(3):
                nxt[sub, c, z] = w[c]


def solution(mesh):
    nx, ny = mesh.shape["gx"], mesh.shape["gy"]
    table, corner = wave_tables(nx, ny)
    base, phase, twist, lanes = trig_tables(nx)
    vmem = pl.BlockSpec(memory_space=pltpu.VMEM)
    hbm = pl.BlockSpec(memory_space=pl.ANY)
    dma = pltpu.SemaphoreType.DMA
    regular = pltpu.SemaphoreType.REGULAR

    def scratch(*shape, dtype=F32):
        return pltpu.VMEM(shape, dtype)

    def on_device(spin_angles, species):
        raw, fld = pl.pallas_call(
            functools.partial(step_kernel, nx, ny, corner),
            out_shape=[
                jax.ShapeDtypeStruct((2, 3, 4, 32, 128), F32),
                jax.ShapeDtypeStruct((16, 128), F32),
            ],
            in_specs=[hbm] * 7,
            out_specs=[vmem] * 2,
            scratch_shapes=[
                scratch(2, PART_K, 128),
                scratch(2, 128),
                scratch(2, nx, 128),
                scratch(2, 128),
                scratch(2, 2, 4, 32, 128),
                scratch(2, 4, 32, 128, dtype=jnp.int32),
                scratch(3, 32, 128),
                scratch(8, 128),
                scratch(nx, 8, 128),
                scratch(256, 128, dtype=BF16),
                scratch(256, 128, dtype=BF16),
                scratch(2, TABLE_ROWS, 128),
                scratch(2, TABLE_ROWS, 128),
                scratch(2, 8, 128),
                scratch(2, 8, 128),
                scratch(2, ny // 2, 2, 8, 128),
                scratch(nx, 16, 128),
                scratch(nx, 16, 128),
                scratch(2, 8, 128),
                scratch(2, 2, 4, 2, 128),
                scratch(2, 4, 2, 128, dtype=jnp.int32),
                scratch(2, 8, 128),
                scratch(2, 2, 8, 128),
                scratch(6, 4, 40, 256),
                scratch(2, 4, 40, 256),
                scratch(2, 3, 4, 40, 256),
                scratch(2, 3, 4, 40, 256),
                scratch(2, 3, 4, 40, 256),
                scratch(3, 40, 256),
                dma((10,)),
                dma, dma, dma, dma((GROUPS,)), dma((GROUPS,)), dma((GROUPS,)), dma, dma,
                dma((4,)),
                dma((4,)),
                regular((3,)),
            ],
            compiler_params=pltpu.CompilerParams(collective_id=0, has_side_effects=True),
        )(spin_angles, species, table, base, phase, twist, lanes)
        return pl.pallas_call(
            finish_kernel,
            out_shape=[
                jax.ShapeDtypeStruct((2, 3, 4, 32, 128), F32),
                jax.ShapeDtypeStruct((3, 1, 8, 32), F32),
            ],
            in_specs=[vmem] * 2,
            out_specs=[vmem] * 2,
        )(raw, fld)

    return jax.shard_map(
        lambda a, s: tuple(on_device(a, s)),
        mesh=mesh,
        in_specs=(P(None, None, None, "gy", "gx"), P(None, None, "gy", "gx")),
        out_specs=(P(None, None, None, "gy", "gx"), P(None, None, "gy", "gx")),
        check_vma=False,
    )
```

```python
import functools
import math

import jax
import jax.numpy as jnp
import numpy as np
from jax import lax
from jax.experimental import pallas as pl
from jax.experimental.pallas import tpu as pltpu
from jax.sharding import PartitionSpec as P

MESH = pl.DeviceIdType.MESH
F32, BF16 = jnp.float32, jnp.bfloat16

CELLS_M = 4
DAMPING = 0.1
TIME_STEP = 0.05
EXCHANGE_SCALE = 0.6
DIPOLE = 2.0
MOMENT_PAIR = (2.22, 1.72)
COUPLING_PAIR = (1.0, 1.25)
ANISOTROPY_PAIR = (0.3, 0.9)
RATIO_PAIR = (COUPLING_PAIR[0] / MOMENT_PAIR[0], COUPLING_PAIR[1] / MOMENT_PAIR[1])
EASY_PAIR = (2 * ANISOTROPY_PAIR[0] / MOMENT_PAIR[0], 2 * ANISOTROPY_PAIR[1] / MOMENT_PAIR[1])

PART_K = 32
ROWS = 8
COLS = 32
GROUPS = 6
WINDOWS = 10
TABLE_LEAD = 8
TABLE_ROWS = 400


def wave_tables(nx, ny):
    period_x, period_y = 2 * nx * COLS, 2 * ny * ROWS
    half_y = period_y // 2
    v = np.arange(period_x // 2 + 1)
    u = np.arange(half_y + 1)
    a = 2 * np.pi * v[:, None] / period_x
    b = 2 * np.pi * u[None, :] / period_y
    k = np.sqrt(a * a + b * b)
    inv = np.where(k > 0, 1.0 / np.where(k > 0, k, 1.0), 0.0)
    g = {
        "xx": -a * a * 0.5 * inv,
        "yy": -b * b * 0.5 * inv,
        "zz": 0.5 * k - 1.0,
        "xy": -a * b * 0.5 * inv,
    }
    dy = np.arange(-TABLE_LEAD, TABLE_ROWS - TABLE_LEAD)
    angle = 2 * np.pi * ((u[:, None] * dy[None, :]) % period_y) / period_y
    fold = np.where((u == 0) | (u == half_y), 1.0, 2.0)
    cosine = fold[:, None] * np.cos(angle)
    sine = np.where((u == 0) | (u == half_y), 0.0, 2.0)[:, None] * np.sin(angle)
    scale = DIPOLE / (period_x * period_y) * np.where((v == 0) | (v == period_x // 2), 1.0, 2.0)
    tables = [scale[:, None] * (g[n] @ cosine) for n in ("xx", "yy", "zz")]
    odd = scale[:, None] * (g["xy"] @ sine)
    odd[-1] = 0.0
    tables.append(odd)
    lanes = np.stack(tables)
    out = np.zeros((nx + 1, TABLE_ROWS, 4 * PART_K), np.float32)
    for s in range(nx):
        block = lanes[:, s * PART_K : (s + 1) * PART_K, :]
        out[s] = block.transpose(2, 0, 1).reshape(TABLE_ROWS, -1)
    out[nx] = out[0]
    for n in range(4):
        out[nx, :, n * PART_K] = lanes[n, -1, :]
    corner = DIPOLE / (period_x * period_y) * float(-0.5 * np.pi * np.pi / np.sqrt(2 * np.pi**2))
    return out, corner


def trig_tables(nx):
    period = 2 * nx * COLS
    lane = np.arange(128)
    comp = np.where(lane < 96, lane // 32, np.where(lane < 102, (lane - 96) // 2, 3))
    place = np.where(lane < 96, lane % 32, np.where(lane % 2 == 0, -1, 32))
    j = np.arange(PART_K)
    t = 2 * np.pi * ((j[:, None] * place[None, :]) % period) / period
    base = np.stack([np.cos(t), np.sin(t)]).astype(np.float32)
    s = np.arange(nx)
    t = 2 * np.pi * ((s[:, None] * PART_K * place[None, :]) % period) / period
    phase = np.stack([np.cos(t), np.sin(t)], axis=1).astype(np.float32)
    jl = lane % 32
    t = 2 * np.pi * ((s[:, None] * COLS * jl[None, :]) % period) / period
    twist = np.stack([np.cos(t), np.sin(t)]).astype(np.float32)
    row = np.stack([comp, np.where(place % 2 == 0, 1, -1)]).astype(np.float32)
    return base, phase, twist, row


def sine(r):
    q = r * r
    p = 1.0 / 6227020800.0
    for c in (-1.0 / 39916800.0, 1.0 / 362880.0, -1.0 / 5040.0, 1.0 / 120.0, -1.0 / 6.0):
        p = p * q + c
    return r + r * q * p


def sine_cosine(x):
    size = jnp.abs(x)
    far = (np.float32(math.pi) - size) + np.float32(math.pi - float(np.float32(math.pi)))
    s = sine(jnp.where(size > np.float32(math.pi / 2), far, size))
    half = (np.float32(math.pi / 2) - size) + np.float32(
        math.pi / 2 - float(np.float32(math.pi / 2))
    )
    return jnp.where(x < 0, -s, s), sine(half)


def pick(cobalt, pair):
    return jnp.where(cobalt, np.float32(pair[1]), np.float32(pair[0]))


def unit(polar, azimuth):
    sp, cp = sine_cosine(polar)
    sq, cq = sine_cosine(azimuth)
    return sp * cq, sp * sq, cp


def iota(shape, dim):
    return lax.broadcasted_iota(jnp.int32, shape, dim)


def cross(a, b):
    return (
        a[1] * b[2] - a[2] * b[1],
        a[2] * b[0] - a[0] * b[2],
        a[0] * b[1] - a[1] * b[0],
    )


def torque(v, h):
    p = cross(v, h)
    r = cross(v, p)
    return [
        (a + np.float32(DAMPING) * b) * np.float32(-1.0 / (1.0 + DAMPING * DAMPING))
        for a, b in zip(p, r)
    ]


def normalized(w):
    s = w[0] * w[0] + w[1] * w[1] + w[2] * w[2]
    r = lax.rsqrt(s)
    r = r * (1.5 - 0.5 * s * r * r)
    return [c * r for c in w]


def split(x, pieces):
    out = []
    for _ in range(pieces):
        out.append(x.astype(BF16))
        x = x - out[-1].astype(F32)
    return out


def dot(a, b, dims=(1, 0)):
    return lax.dot_general(
        a, b, (((dims[0],), (dims[1],)), ((), ())), preferred_element_type=F32
    )


def exact_dot(a, hot):
    n = a.shape[0]
    out = dot(jnp.concatenate(split(a, 3), axis=0), hot)
    return out[0:n] + out[n : 2 * n] + out[2 * n : 3 * n]


def wide_dot(a, b_high, b_low, dims):
    n = a.shape[0]
    high, low = split(a, 2)
    out = dot(jnp.concatenate([high, low], axis=0), b_high, dims)
    return out[0:n] + out[n : 2 * n] + dot(high, b_low, dims)


def step_kernel(
    nx, ny, corner,
    ang_hbm, spc_hbm, table_hbm, base_hbm, phase_hbm, twist_hbm, lanes_hbm,
    nxt, fld,
    base, phase, twist, lanes, ang, spc, mom, tile, b_a, q_high, q_low, tab, tab2, up, dn, b_b, send_c, b_c, pack, g_ang, g_spc, g_x, g_c,
    raw, cpl, vec, wgt, fix, dpl,
    load_sem, s_a, r_a, s_b, r_b, s_f, r_f, s_c, r_c, s_h, r_h, word,
):
    gx, gy = lax.axis_index("gx"), lax.axis_index("gy")
    left, right = lax.rem(gx + nx - 1, nx), lax.rem(gx + 1, nx)
    below, above = lax.rem(gy + ny - 1, ny), lax.rem(gy + 1, ny)
    core = lax.rem(gy, 2)
    chip = gy // 2
    partner = gy + 1 - 2 * core
    chips = ny // 2
    nz = ny // 4
    hops = nz // 2
    side, z_own = chip // nz, lax.rem(chip, nz)

    def at(across, dz):
        there = (1 - side) if across else side
        return 2 * (nz * there + lax.rem(z_own + dz + nz, nz)) + core

    group = chips // GROUPS

    loads = []
    for sub in range(2):
        loads.append(pltpu.make_async_copy(ang_hbm.at[sub], ang.at[sub], load_sem.at[2 * sub]))
        loads.append(pltpu.make_async_copy(spc_hbm.at[sub], spc.at[sub], load_sem.at[2 * sub + 1]))
    late_loads = [
        pltpu.make_async_copy(table_hbm.at[gx], tab.at[0], load_sem.at[4]),
        pltpu.make_async_copy(table_hbm.at[jnp.where(gx == 0, nx, gx)], tab.at[1], load_sem.at[5]),
    ]
    small_loads = [
        pltpu.make_async_copy(src, dst, load_sem.at[6 + n])
        for n, (src, dst) in enumerate(
            ((base_hbm, base), (phase_hbm.at[gx], phase), (lanes_hbm, lanes), (twist_hbm, twist))
        )
    ]
    for load in small_loads + loads + late_loads:
        load.start()

    barrier = pltpu.get_barrier_semaphore()

    def signal(semaphore, device):
        pl.semaphore_signal(semaphore, inc=1, device_id=device, device_id_type=MESH)

    @pl.loop(1, nx)
    def _(o):
        signal(barrier, (lax.rem(gx + o, nx), gy))

    near = [above, below, at(True, 0), at(True, 1), at(True, -1)]
    for dz in range(1, hops):
        near += [at(False, dz), at(False, -dz)]
    for other in near:
        signal(barrier, (gx, other))

    def remote(src, dst, send, recv, device):
        return pltpu.make_async_remote_copy(
            src_ref=src, dst_ref=dst, send_sem=send, recv_sem=recv, device_id=device, device_id_type=MESH
        )

    for load in small_loads:
        load.wait()
    b_cos, b_sin = base[0], base[1]
    p_cos, p_sin = phase[0:1, :], phase[1:2, :]
    cosine = b_cos * p_cos - b_sin * p_sin
    sinus = b_sin * p_cos + b_cos * p_sin
    comp, parity = lanes[0:1, :], lanes[1:2, :]
    single = (iota((32, 128), 0) + gx) == 0

    def store_q(at, q):
        q_high[pl.ds(at, 32), :], q_low[pl.ds(at, 32), :] = split(q, 2)

    for c in range(3):
        mine = comp == np.float32(c)
        real, imag = (sinus, cosine) if c == 1 else (cosine, -sinus)
        store_q(32 * c, jnp.where(mine, jnp.where(single, 1.0, real), 0.0))
        store_q(128 + 32 * c, jnp.where(mine, jnp.where(single, parity, imag), 0.0))
    store_q(96, jnp.zeros((32, 128), F32))
    store_q(224, jnp.zeros((32, 128), F32))

    def far_first(o):
        return 1 + lax.rem(o + nx // 2 - 2, nx - 1)

    total = [jnp.zeros((32, 128), F32) for _ in range(3)]
    for sub in range(2):
        loads[2 * sub].wait()
        loads[2 * sub + 1].wait()
        for z in range(4):
            moment = pick(spc[sub, z] == 1, MOMENT_PAIR)
            v = unit(ang[sub, 0, z], ang[sub, 1, z])
            for c in range(3):
                vec[sub, c, z, 0:32, 0:128] = v[c]
            total = [t + moment * c for t, c in zip(total, v)]
    rows = []
    for c in range(3):
        mom[c] = total[c]
        line = mom[c, pl.ds(0, 8, 4), :]
        for r in range(1, 4):
            line = line + mom[c, pl.ds(r, 8, 4), :]
        rows.append(line)
    atom = iota((384, 128), 0)
    place = ((atom >> 7) << 5) + ((atom & 127) >> 2)
    spread = jnp.where(iota((384, 128), 1) == place, 1 / 128, 0.0).astype(BF16)
    packed = exact_dot(jnp.concatenate(rows, axis=1), spread)
    tile[...] = packed

    pl.semaphore_wait(barrier, nx - 1 + len(near))

    @pl.loop(1, nx)
    def _(o):
        to = lax.rem(gx + far_first(o), nx)
        remote(tile, b_a.at[gx], s_a, r_a, (to, gy)).start()

    signal(word.at[0], (gx, at(True, 0)))
    signal(word.at[1], (gx, at(False, -1)))
    signal(word.at[2], (gx, at(True, -1)))

    halo_row, halo_spc, halo_x, halo_c = [
        [remote(src, dst, s_h.at[n], r_h.at[n], to) for src, dst, to in pair]
        for n, pair in enumerate((
            ((ang.at[:, :, :, pl.ds(31, 1), :], g_ang.at[:, :, :, pl.ds(0, 1), :], (gx, above)),
             (ang.at[:, :, :, pl.ds(0, 1), :], g_ang.at[:, :, :, pl.ds(1, 1), :], (gx, below))),
            ((spc.at[:, :, pl.ds(31, 1), :], g_spc.at[:, :, pl.ds(0, 1), :], (gx, above)),
             (spc.at[:, :, pl.ds(0, 1), :], g_spc.at[:, :, pl.ds(1, 1), :], (gx, below))),
            ((pack.at[1], g_x.at[0], (right, gy)), (pack.at[0], g_x.at[1], (left, gy))),
            ((g_x, g_c.at[0], (gx, above)), (g_x, g_c.at[1], (gx, below))),
        ))
    ]
    halo_all = [remote(g, g, s_h.at[n], r_h.at[n], (gx, gy)) for n, g in enumerate((g_ang, g_spc, g_x, g_c))]

    b_a[gx] = packed

    lane = iota((128, 128), 1)
    edges = jnp.zeros((128, 128), F32)
    for q in range(3):
        for sub in range(2):
            n = 2 * q + sub
            block = ang[sub, q] if q < 2 else spc[sub].astype(F32)
            block = block.reshape(128, 128)
            edges = jnp.where(lane == n, pltpu.roll(block, n, 1) if n else block, edges)
            edges = jnp.where(lane == 8 + n, pltpu.roll(block, n + 9, 1), edges)
    edges = jnp.transpose(edges)
    pack[0] = edges[0:8]
    pack[1] = edges[8:16]
    for copy in halo_x + halo_row + halo_spc:
        copy.start()

    def blocks(ref, n, send, recv):
        return remote(ref.at[pl.ds(0, n)], ref.at[pl.ds(0, n)], send, recv, (gx, gy))

    blocks(b_a, nx - 1, s_a, r_a).wait_recv()

    wave = wide_dot(b_a[...].reshape(nx * 8, 128), q_high[...], q_low[...], (1, 1))
    real = jnp.zeros((8, 128), F32)
    imag = jnp.zeros((8, 128), F32)
    for g in range(nx):
        t_re, t_im = wave[8 * g : 8 * g + 8, 0:128], wave[8 * g : 8 * g + 8, 128:256]
        c, s = twist[0, g : g + 1, :], twist[1, g : g + 1, :]
        real = real + (t_re * c + t_im * s)
        imag = imag + (t_im * c - t_re * s)

    lane8 = iota((8, 128), 1)
    is_y = (lane8 >= 32) & (lane8 < 64)
    flip = jnp.where(is_y, np.float32(-1), np.float32(1))
    dn[0] = real * flip
    dn[1] = imag * flip
    for r in range(8):
        up[0, r : r + 1, :] = real[7 - r : 8 - r]
        up[1, r : r + 1, :] = imag[7 - r : 8 - r]

    for n in range(3):
        pl.semaphore_wait(word.at[n], 1)

    @pl.loop(0, chips - 1)
    def _(k):
        slot = chips - 1 - k
        n, a = slot // 2, lax.rem(slot, 2)
        odd = lax.rem(n, 2) == 1
        steps = jnp.where(odd, (n + 1) // 2, nz - n // 2)
        back = jnp.where((n == 0) | (n == nz - 1), n, jnp.where(odd, n + 1, n - 1))
        there = 2 * back + a
        to_chip = nz * jnp.where(a == 1, 1 - side, side) + lax.rem(z_own + steps, nz)
        to = 2 * to_chip + core
        land, mark = b_b.at[core, there], r_b.at[there // group]

        @pl.when(to > gy)
        def _():
            remote(up, land, s_b, mark, (gx, to)).start()

        @pl.when(to < gy)
        def _():
            remote(dn, land, s_b, mark, (gx, to)).start()

    even = core == 0
    b_b[core, 0] = jnp.where(even, up[...], dn[...])

    for load in late_loads:
        load.wait()
    wide = iota((TABLE_ROWS, 128), 1)
    for p in range(2):
        t = tab[p]
        tab2[p] = jnp.where(
            wide < 32,
            pltpu.roll(t, 32, 1),
            jnp.where(wide < 64, -pltpu.roll(t, 64, 1), 0.0),
        )

    halo_all[2].wait_recv()
    for copy in halo_c:
        copy.start()
    halo_all[0].wait_recv()
    halo_all[1].wait_recv()
    halo_all[3].wait_recv()

    cols = jnp.concatenate(
        [g_x[0], g_x[1], g_c[0, 0], g_c[0, 1], g_c[1, 0], g_c[1, 1], jnp.zeros((80, 128), F32)], axis=0
    )
    cols = jnp.transpose(cols)
    lane32 = iota((32, 128), 1)
    rowh = iota((8, 128), 0)
    for q in range(3):
        for sub in range(2):
            n = 2 * q + sub
            for z in range(4):

                def column(piece):
                    part = cols[32 * z : 32 * z + 32, 8 * piece + n : 8 * piece + n + 1]
                    return jnp.broadcast_to(part, (32, 128))

                def spot(piece, y):
                    part = cols[32 * z + y : 32 * z + y + 1, 8 * piece + n : 8 * piece + n + 1]
                    return jnp.broadcast_to(part, (8, 128))

                def edge(side):
                    if q < 2:
                        return jnp.broadcast_to(g_ang[sub, q, z, side : side + 1, :], (8, 128))
                    return jnp.broadcast_to(g_spc[sub, z, side : side + 1, :], (8, 128)).astype(F32)

                if q == 2:
                    raw[n, z, 0:32, 0:128] = spc[sub, z].astype(F32)
                raw[n, z, 0:32, 128:256] = jnp.where(lane32 < 64, column(1), column(0))
                raw[n, z, 32:40, 0:128] = jnp.where(rowh < 4, edge(1), edge(0))
                low = jnp.where(lane8 < 64, spot(3, 31), spot(2, 31))
                high = jnp.where(lane8 < 64, spot(5, 0), spot(4, 0))
                raw[n, z, 32:40, 128:256] = jnp.where(rowh < 4, high, low)

    at_row = iota((40, 256), 0)
    at_col = iota((40, 256), 1)
    y = gy * 32 + jnp.where(at_row < 36, at_row, at_row - 40)
    x = gx * 128 + jnp.where(at_col < 192, at_col, at_col - 256)
    inside = (y >= 0) & (y < ny * 32) & (x >= 0) & (x < nx * 128)
    for sub in range(2):
        for z in range(4):
            for r, l in ((slice(0, 32), slice(128, 256)), (slice(32, 40), slice(0, 256))):
                v = unit(raw[sub, z, r, l], raw[2 + sub, z, r, l])
                for c in range(3):
                    vec[sub, c, z, r, l] = v[c]
            coupling = jnp.where(inside, pick(raw[4 + sub, z] > 0.5, COUPLING_PAIR), 0.0)
            cpl[sub, z] = coupling
            for c in range(3):
                wgt[sub, c, z] = coupling * vec[sub, c, z]

    def neighbours(sub, c, z):
        other = 1 - sub
        near = wgt[other, c, z]
        far = z - 1 if sub == 0 else z + 1
        if 0 <= far < 4:
            near = near + wgt[other, c, far]
        near = near + pltpu.roll(near, 1 if sub == 0 else 255, 1)
        return near + pltpu.roll(near, 1 if sub == 0 else 39, 0)

    ratio_pair = [np.float32(EXCHANGE_SCALE) * np.float32(r) for r in RATIO_PAIR]
    for sub in range(2):
        for z in range(4):
            cobalt = raw[4 + sub, z] > 0.5
            ratio = pick(cobalt, ratio_pair)
            for c in range(3):
                h = ratio * neighbours(sub, c, z)
                if c == 2:
                    h = h + pick(cobalt, EASY_PAIR) * vec[sub, c, z]
                fix[sub, c, z] = h

    def hand_on(g):
        part = b_b.at[core, pl.ds(group * g, group)]
        return remote(part, part, s_f.at[g], r_f.at[g], (gx, partner))

    for g in range(GROUPS):
        blocks(b_b.at[core], group - (g == 0), s_b, r_b.at[g]).wait_recv()
        hand_on(g).start()

    zero = jnp.zeros((8, 128), F32)

    def swapped(s):
        return jnp.where(lane8 < 32, pltpu.roll(s, 96, 1), pltpu.roll(s, 32, 1))

    def add_source(d, parts, acc):
        acc = list(acc)
        for p in range(2):
            s = parts[p]
            t = swapped(s)
            for w in range(WINDOWS):
                span = pl.ds(8 * d + w, 8)
                acc[2 * w + p] = acc[2 * w + p] + tab[p, span, :] * s + tab2[p, span, :] * t
        acc[-1] = acc[-1] + parts[1]
        return tuple(acc)

    def add_chips(which, acc_up, acc_dn):
        def source(k):
            ahead = lax.rem(lax.rem(k, nz) - z_own + nz, nz)
            n = jnp.where(
                ahead == 0, 0, jnp.where(ahead <= hops, 2 * ahead - 1, 2 * (nz - ahead))
            )
            slot = 2 * n + jnp.where(k // nz == side, 0, 1)
            return b_b[which, slot, 0], b_b[which, slot, 1]

        acc_up = lax.fori_loop(
            0, chip, lambda k, a: add_source(gy - (2 * k + which), source(k), a), acc_up
        )
        acc_dn = lax.fori_loop(
            chip + 1, chips, lambda k, a: add_source(2 * k + which - gy, source(k), a), acc_dn
        )
        return acc_up, acc_dn

    start = tuple(zero for _ in range(2 * WINDOWS + 1))
    acc_up = add_source(0, (up[0], up[1]), start)
    acc_up, acc_dn = add_chips(core, acc_up, start)
    for g in range(GROUPS):
        hand_on(g).wait_recv()
    acc_up, acc_dn = add_chips(1 - core, acc_up, acc_dn)
    beside = (b_b[1 - core, 0, 0], b_b[1 - core, 0, 1])
    acc_up = lax.fori_loop(0, core, lambda _, a: add_source(1, beside, a), acc_up)
    acc_dn = lax.fori_loop(0, 1 - core, lambda _, a: add_source(1, beside, a), acc_dn)

    alternate = jnp.where(iota((8, 128), 0) % 2 == 0, np.float32(1), np.float32(-1))
    last = jnp.sum((flip * acc_dn[-1] - acc_up[-1]) * alternate, axis=0, keepdims=True)
    last = jnp.broadcast_to(last, (8, 128))
    last = swapped(last)
    last = jnp.where(((lane8 == 0) | (lane8 == 32)) & (gx == 0), last, 0.0) * np.float32(corner)

    row16 = iota((16, 128), 0)
    field = []
    for p in range(2):
        out = jnp.zeros((16, 128), F32)
        for w in range(WINDOWS):
            sums = acc_up[2 * w + p] + flip * acc_dn[2 * (WINDOWS - 1 - w) + p]
            if p == 1:
                sign = np.float32((1 if w % 2 else -1) / 8)
                sums = sums + sign * last
            line = jnp.sum(sums, axis=0, keepdims=True)
            out = jnp.where(row16 == w, jnp.broadcast_to(line, (16, 128)), out)
        field.append(out)

    turned = []
    for g in range(nx):
        c, s = twist[0, g : g + 1, :], twist[1, g : g + 1, :]
        turned.append(
            jnp.concatenate([field[0] * c - field[1] * s, field[0] * s + field[1] * c], axis=1)
        )
    shares = wide_dot(jnp.concatenate(turned, axis=0), q_high[...], q_low[...], (1, 0))
    send_c[...] = shares.reshape(nx, 16, 128)

    @pl.loop(1, nx)
    def _(o):
        to = lax.rem(gx + far_first(o), nx)
        part = pl.ds(0, WINDOWS)
        remote(send_c.at[to, part], b_c.at[gx, part], s_c, r_c, (to, gy)).start()

    b_c[gx] = send_c[gx]
    atom = iota((128, 256), 1)
    want = jnp.where(atom < 128, atom >> 2, jnp.where(atom < 192, 97, 96))
    scale = jnp.where(atom < 128, 32, 2)
    hot = [
        jnp.where(iota((128, 256), 0) == want + scale * c, 1.0, 0.0).astype(BF16) for c in range(3)
    ]
    row8 = iota((8, 256), 0)

    all_c = b_c.at[pl.ds(0, nx - 1), pl.ds(0, WINDOWS)]
    shares_in = remote(all_c, all_c, s_c, r_c, (gx, gy))
    shares_in.wait_recv()
    whole = b_c[0]
    for g in range(1, nx):
        whole = whole + b_c[g]

    fld[...] = whole
    for c in range(3):
        lines = exact_dot(whole, hot[c])

        def line(w):
            return jnp.broadcast_to(lines[w : w + 1], (8, 256))

        for t in range(4):
            dpl[c, pl.ds(8 * t, 8), :] = jnp.where(row8 < 4, line(2 * t + 1), line(2 * t + 2))
        dpl[c, pl.ds(32, 8), :] = jnp.where(row8 < 4, line(9), line(0))

    for sub in range(2):
        for z in range(4):
            v = [vec[sub, c, z] for c in range(3)]
            f = torque(v, [fix[sub, c, z] + dpl[c] for c in range(3)])
            p = normalized([a + np.float32(TIME_STEP) * b for a, b in zip(v, f)])
            coupling = cpl[sub, z]
            for c in range(3):
                wgt[sub, c, z] = coupling * p[c]
                fix[sub, c, z, 0:32, 0:128] = p[c][0:32, 0:128]
                nxt[sub, c, z] = f[c][0:32, 0:128]
    for sub in range(2):
        for z in range(4):
            cobalt = spc[sub, z] == 1
            ratio = pick(cobalt, ratio_pair)
            p = [fix[sub, c, z, 0:32, 0:128] for c in range(3)]
            h = [
                ratio * neighbours(sub, c, z)[0:32, 0:128] + dpl[c, 0:32, 0:128] for c in range(3)
            ]
            h[2] = h[2] + pick(cobalt, EASY_PAIR) * p[2]
            f = torque(p, h)
            w = [
                vec[sub, c, z, 0:32, 0:128] + np.float32(0.5 * TIME_STEP) * (nxt[sub, c, z] + f[c])
                for c in range(3)
            ]
            for c in range(3):
                nxt[sub, c, z] = w[c]

    for halo in halo_all:
        halo.wait_send()
    blocks(b_a, nx - 1, s_a, r_a).wait_send()
    shares_in.wait_send()
    blocks(b_b.at[core], chips - 1, s_b, r_b.at[0]).wait_send()
    for g in range(GROUPS):
        hand_on(g).wait_send()


def finish_kernel(raw, fld, nxt, dip):
    for c in range(3):
        dip[c, 0] = fld[1:9, 32 * c : 32 * c + 32]
    for sub in range(2):
        for z in range(4):
            w = normalized([raw[sub, c, z] for c in range(3)])
            for c in range(3):
                nxt[sub, c, z] = w[c]


def solution(mesh):
    nx, ny = mesh.shape["gx"], mesh.shape["gy"]
    table, corner = wave_tables(nx, ny)
    base, phase, twist, lanes = trig_tables(nx)
    vmem = pl.BlockSpec(memory_space=pltpu.VMEM)
    hbm = pl.BlockSpec(memory_space=pl.ANY)
    dma = pltpu.SemaphoreType.DMA
    regular = pltpu.SemaphoreType.REGULAR

    def scratch(*shape, dtype=F32):
        return pltpu.VMEM(shape, dtype)

    def on_device(spin_angles, species):
        raw, fld = pl.pallas_call(
            functools.partial(step_kernel, nx, ny, corner),
            out_shape=[
                jax.ShapeDtypeStruct((2, 3, 4, 32, 128), F32),
                jax.ShapeDtypeStruct((16, 128), F32),
            ],
            in_specs=[hbm] * 7,
            out_specs=[vmem] * 2,
            scratch_shapes=[
                scratch(2, PART_K, 128),
                scratch(2, 128),
                scratch(2, nx, 128),
                scratch(2, 128),
                scratch(2, 2, 4, 32, 128),
                scratch(2, 4, 32, 128, dtype=jnp.int32),
                scratch(3, 32, 128),
                scratch(8, 128),
                scratch(nx, 8, 128),
                scratch(256, 128, dtype=BF16),
                scratch(256, 128, dtype=BF16),
                scratch(2, TABLE_ROWS, 128),
                scratch(2, TABLE_ROWS, 128),
                scratch(2, 8, 128),
                scratch(2, 8, 128),
                scratch(2, ny // 2, 2, 8, 128),
                scratch(nx, 16, 128),
                scratch(nx, 16, 128),
                scratch(2, 8, 128),
                scratch(2, 2, 4, 2, 128),
                scratch(2, 4, 2, 128, dtype=jnp.int32),
                scratch(2, 8, 128),
                scratch(2, 2, 8, 128),
                scratch(6, 4, 40, 256),
                scratch(2, 4, 40, 256),
                scratch(2, 3, 4, 40, 256),
                scratch(2, 3, 4, 40, 256),
                scratch(2, 3, 4, 40, 256),
                scratch(3, 40, 256),
                dma((10,)),
                dma, dma, dma, dma((GROUPS,)), dma((GROUPS,)), dma((GROUPS,)), dma, dma,
                dma((4,)),
                dma((4,)),
                regular((3,)),
            ],
            compiler_params=pltpu.CompilerParams(collective_id=0, has_side_effects=True),
        )(spin_angles, species, table, base, phase, twist, lanes)
        return pl.pallas_call(
            finish_kernel,
            out_shape=[
                jax.ShapeDtypeStruct((2, 3, 4, 32, 128), F32),
                jax.ShapeDtypeStruct((3, 1, 8, 32), F32),
            ],
            in_specs=[vmem] * 2,
            out_specs=[vmem] * 2,
        )(raw, fld)

    return jax.shard_map(
        lambda a, s: tuple(on_device(a, s)),
        mesh=mesh,
        in_specs=(P(None, None, None, "gy", "gx"), P(None, None, "gy", "gx")),
        out_specs=(P(None, None, None, "gy", "gx"), P(None, None, "gy", "gx")),
        check_vma=False,
    )
```
